32 devices in a mesh: ta: 4 (over x, core), au: 8 (over z, y).
Axes of the slice: x: 2, y: 2, z: 4, core: 2. Of those that a mesh axis runs over, the one named last changes fastest.
Arguments:
- embeddings: bfloat16 [786432, 192], P(('ta', 'au')), may hold values from -6 to 6
- stream_ids: int32 [786432], P(('ta', 'au')), may hold values from 0 to 63, never falling along the last dimension, each value on 1 to 24576 neighbouring positions
- start_block: bfloat16 [786432, 64], P(('ta', 'au')), may hold values from -6 to 6
Outputs:
- basis_rows: float32 [786432, 64], P(('ta', 'au'))
- ritz_matrix: float32 [64, 64], replicated
The draws below stay inside these ranges and needn't reach their ends.
Inputs may be any that keep to these rules, and one draw needn't show every extreme that they name: stream_ids never fall along the rows; each stream holds 1 to 24576 rows.
All inputs are finite; a program needn't handle non-finite values.
Results may differ from the reference program's by a relative error of at most 0.0015.
Values may be sent and summed in bfloat16 or wider, within the bound.
No kernel may reach another device: no remote copies, remote signals or barrier semaphores. Data moves between devices by JAX's collectives and lax.ppermute only.
A program may use at most 192 MiB of HBM per device.

```python
import math
import jax
import jax.numpy as jnp
import numpy as np
from jax import lax

EMB = 192
VECS = 64
BAND = 128
ROWS_DEV = 24576
ROWS = 786432
STREAMS = 64


def block_scale(stream_key, dims, pieces, least, largest):
    def one(dim, shards_of):
        draws = jax.random.uniform(jax.random.fold_in(jax.random.fold_in(stream_key, 6), dim), (shards_of,), jnp.float32, least / len(pieces), largest / len(pieces))
        return jnp.repeat(jnp.exp(draws), dims[dim] // shards_of).reshape((-1,) + (1,) * (len(dims) - dim - 1))

    level = one(*pieces[0])
    for cut in pieces[1:]:
        level = level * one(*cut)
    return level


def length_profile(count, total, most, lean):
    portions = [(1 << 20) // math.isqrt(grade ** lean) + 1 for grade in range(2, count + 1)]
    surplus, counts = total - most - (count - 1), [1] * (count - 1)
    while surplus > 0:
        movable = [i for i in range(count - 1) if counts[i] < most]
        mass, remaining = sum([portions[i] for i in movable]), surplus
        for i in movable:
            extra = min(most - counts[i], max(1, remaining * portions[i] // mass), surplus)
            counts[i] = counts[i] + extra
            surplus = surplus - extra
    return np.array([most] + counts)


def ragged(stream_key, number_of, total, limit, skew):
    if number_of == 2:
        one = jax.random.randint(stream_key, (), max(1, total - limit), min(limit, total - 1) + 1)
        return jnp.stack([one, total - one])
    tallies = jnp.asarray(length_profile(number_of, total, limit, skew), jnp.int32)
    couples = (number_of - 1) // 2
    giver, sink = tallies[1:1 + 2 * couples:2], tallies[2:2 + 2 * couples:2]
    slack = jnp.minimum(giver - 1, limit - sink)
    shifted = jax.random.randint(jax.random.fold_in(stream_key, 1), (couples,), 0, 1 << 20) % (slack + 1)
    tallies = tallies.at[1:1 + 2 * couples:2].set(giver - shifted).at[2:2 + 2 * couples:2].set(sink + shifted)
    return tallies[jax.random.permutation(jax.random.fold_in(stream_key, 2), number_of)]


def normal_values(stream_key, extent, spread, most, pieces=(), kind=jnp.bfloat16):
    values = spread * jax.random.normal(stream_key, extent, jnp.float32)
    if pieces:
        values = values * block_scale(stream_key, extent, pieces, -0.22, 0.18)
    return jnp.clip(values, -most, most).astype(kind)


def setup_inputs(seed: int = 0) -> dict:
    key_list = jax.random.split(jax.random.key(seed), 4)
    embeddings = normal_values(key_list[0], (ROWS, EMB), 1.0, 6.0, ((0, 32),))
    stream_ids = jnp.searchsorted(jnp.cumsum(ragged(key_list[1], STREAMS, ROWS, ROWS_DEV, 1)), jnp.arange(ROWS), side="right").astype(jnp.int32)
    start_block = normal_values(key_list[2], (ROWS, VECS), 1.0, 6.0, ((0, 32),))
    return {"embeddings": embeddings, "stream_ids": stream_ids, "start_block": start_block}


sharpness = 3.0
center_value = 0.3
half_range = 0.6

def normalized_rows(embeddings):
    values = embeddings.astype(jnp.float32)
    return (values * lax.rsqrt(lax.optimization_barrier(jnp.sum(values * values, axis=-1, keepdims=True)) + 1e-06)).astype(jnp.bfloat16)

def band_tiles(normed_ext, label_ext):
    tile_total = normed_ext.shape[0] // BAND - 2
    tiled_layout = normed_ext.reshape(tile_total + 2, BAND, -1)
    segment_windows = jnp.concatenate([tiled_layout[:-2], tiled_layout[1:-1], tiled_layout[2:]], axis=1)
    cosine_affinity = jnp.einsum('uod,uqd->uoq', tiled_layout[1:-1].astype(jnp.float32), segment_windows.astype(jnp.float32))
    label_view = label_ext.reshape(tile_total + 2, BAND)
    label_win = jnp.concatenate([label_view[:-2], label_view[1:-1], label_view[2:]], axis=1)
    same_stream = label_view[1:-1][:, :, None] == label_win[:, None, :]
    row_pos = jnp.arange(BAND, dtype=jnp.int32)
    col_pos = jnp.arange(3 * BAND, dtype=jnp.int32)
    inside_diagonal_band = jnp.abs(col_pos[None, :] - BAND - row_pos[:, None]) <= BAND
    weights = jnp.where(same_stream & inside_diagonal_band[None], jnp.exp(sharpness * (cosine_affinity - 1.0)), 0.0).astype(jnp.bfloat16)
    degree = lax.optimization_barrier(jnp.sum(weights.astype(jnp.float32), axis=-1))
    return (weights, degree)

def band_product(weights, packed_ext):
    tile_total = weights.shape[0]
    tiled_layout = packed_ext.reshape(tile_total + 2, BAND, -1)
    segment_windows = jnp.concatenate([tiled_layout[:-2], tiled_layout[1:-1], tiled_layout[2:]], axis=1)
    product = jnp.einsum('trc,tcv->trv', weights.astype(jnp.float32), segment_windows.astype(jnp.float32))
    return product.reshape(tile_total * BAND, -1)

def reference(embeddings, stream_ids, start_block):
    tile_count = ROWS_DEV // BAND
    groups = jnp.arange(ROWS // ROWS_DEV, dtype=jnp.int32)
    normed = normalized_rows(embeddings)
    padded_unit = jnp.pad(normed, ((BAND, BAND), (0, 0)))
    padded_label = jnp.pad(stream_ids + 1, (BAND, BAND))

    def affinity_group(group_index):
        start = (group_index * ROWS_DEV).astype(jnp.int32)
        part_unit = lax.dynamic_slice_in_dim(padded_unit, start, ROWS_DEV + 2 * BAND, 0)
        part_label = lax.dynamic_slice_in_dim(padded_label, start, ROWS_DEV + 2 * BAND, 0)
        return band_tiles(part_unit, part_label)
    weights, degree = lax.map(affinity_group, groups)
    scale_factors = lax.rsqrt(degree).reshape(ROWS, 1)

    def apply_operator(level):
        packed = (scale_factors * level).astype(jnp.bfloat16)
        padded = jnp.pad(packed, ((BAND, BAND), (0, 0)))

        def group_apply_step(group_index):
            start = (group_index * ROWS_DEV).astype(jnp.int32)
            part = lax.dynamic_slice_in_dim(padded, start, ROWS_DEV + 2 * BAND, 0)
            return band_product(weights[group_index], part)
        return scale_factors * lax.map(group_apply_step, groups).reshape(ROWS, -1)
    level0 = start_block.astype(jnp.float32)
    level1 = (apply_operator(level0) - center_value * level0) / half_range
    level2 = 2.0 * (apply_operator(level1) - center_value * level1) / half_range - level0
    level3 = 2.0 * (apply_operator(level2) - center_value * level2) / half_range - level1
    image_block = apply_operator(level3)
    gram_part = jnp.einsum('rv,rw->vw', level3, level3, precision=lax.Precision.HIGHEST)
    image_part = jnp.einsum('rv,rw->vw', level3, image_block, precision=lax.Precision.HIGHEST)
    factor = jnp.linalg.cholesky(gram_part)
    basis_rows = jax.scipy.linalg.solve_triangular(factor, level3.T, lower=True).T
    left_solved = jax.scipy.linalg.solve_triangular(factor, image_part, lower=True)
    ritz_matrix = jax.scipy.linalg.solve_triangular(factor, left_solved.T, lower=True).T
    return (basis_rows, ritz_matrix)
```

```python
import jax
import jax.numpy as jnp
from jax import lax
from jax.experimental import pallas as pl
from jax.experimental.pallas import tpu as pltpu
from jax.sharding import PartitionSpec as P

BAND = 128
HALO_BLOCKS = 5
HALO = HALO_BLOCKS * BAND
EMB = 192
VECS = 64
CHUNK_BLOCKS = 16
CHUNK = CHUNK_BLOCKS * BAND
DEPTH = 256
PENALTY = 64.0
EXPONENT = 4.328085122666891
VMEM_BYTES = 62 << 20

bf16 = jnp.bfloat16
f32 = jnp.float32


def columns(start, size):
    return pl.ds(pl.multiple_of(start, BAND), size)


def split(x):
    high = x.astype(bf16)
    return high, (x - high.astype(f32)).astype(bf16)


def prepare(values, labels, slot, lhs_ref, rhs_ref):
    width = values.shape[1]
    values = values.astype(f32)
    normed = (values * lax.rsqrt(jnp.sum(values * values, axis=0, keepdims=True) + 1e-06)).astype(bf16)
    shift = lax.broadcasted_iota(jnp.int32, (16, width), 0)
    bits = (lax.shift_right_logical(jnp.broadcast_to(labels, (16, width)), shift) & 1).astype(f32)
    unset = 1.0 - bits
    first = jnp.where(shift == 0, 1.0, 0.0)
    zeros = jnp.zeros((16, width), bf16)
    rhs = jnp.concatenate(
        [normed, (-PENALTY * unset).astype(bf16), (-PENALTY * bits).astype(bf16), (-first).astype(bf16), zeros], axis=0
    )
    lhs = jnp.concatenate([normed, bits.astype(bf16), unset.astype(bf16), first.astype(bf16), zeros], axis=0)
    rhs_ref[:, slot * BAND : slot * BAND + width] = rhs
    lhs_ref[slot * BAND : slot * BAND + width, :] = lhs.T


def affinity_pair(slot, block, carried, right, lhs_ref, rhs_ref, weight_ref, scale_ref):
    row = lax.broadcasted_iota(jnp.int32, (BAND, BAND), 0)
    col = lax.broadcasted_iota(jnp.int32, (BAND, BAND), 1)
    here = slice(slot * BAND, (slot + 2) * BAND)
    z = jnp.dot(lhs_ref[here, :], rhs_ref[:, here], preferred_element_type=f32)
    e = jnp.exp2(z * EXPONENT)
    own0 = e[:BAND, :BAND].astype(bf16)
    own1 = e[BAND:, BAND:].astype(bf16)
    right0 = jnp.where(row <= col, e[BAND:, :BAND], 0.0).astype(bf16)
    left1 = jnp.where(row >= col, e[:BAND, BAND:], 0.0).astype(bf16)
    weight_ref[block, BAND : 2 * BAND, :] = own0
    weight_ref[block, 2 * BAND :, :] = right0
    weight_ref[block + 1, :BAND, :] = left1
    weight_ref[block + 1, BAND : 2 * BAND, :] = own1
    sum0 = jnp.sum(own0.astype(f32) + right0.astype(f32), axis=0, keepdims=True) + carried
    scale_ref[:, columns(block * BAND, BAND)] = lax.rsqrt(sum0)
    if not right:
        return carried
    z = jnp.dot(
        lhs_ref[(slot + 2) * BAND : (slot + 3) * BAND, :],
        rhs_ref[:, (slot + 1) * BAND : (slot + 2) * BAND],
        preferred_element_type=f32,
    )
    right1 = jnp.where(row <= col, jnp.exp2(z * EXPONENT), 0.0).astype(bf16)
    left2 = right1.T
    weight_ref[block + 1, 2 * BAND :, :] = right1
    weight_ref[block + 2, :BAND, :] = left2
    sum1 = jnp.sum(own1.astype(f32) + left1.astype(f32) + right1.astype(f32), axis=0, keepdims=True)
    scale_ref[:, columns(block * BAND + BAND, BAND)] = lax.rsqrt(sum1)
    return jnp.sum(left2.astype(f32), axis=0, keepdims=True)


def filter_kernel(
    low_ref, high_ref, emb_ref, id_ref, start_hbm,
    level_hbm, gram_ref,
    lhs_ref, rhs_ref, weight_ref, scale_ref, carry_ref, start_ref, pack_a, pack_b, level_a, level_b, sum_ref, sems,
):
    step = pl.program_id(0)
    count = pl.num_programs(0)
    rows = count * CHUNK
    blocks = rows // BAND
    start_copy = pltpu.make_async_copy(start_hbm, start_ref.at[:, HALO : HALO + start_hbm.shape[1]], sems.at[0])

    def pairs(first_slot, first_block, number, last_right):
        carried = carry_ref[...]
        for i in range(number):
            right = last_right or i < number - 1
            carried = affinity_pair(
                first_slot + 2 * i, first_block + 2 * i, carried, right, lhs_ref, rhs_ref, weight_ref, scale_ref
            )
        carry_ref[...] = carried

    def halo(ref, slot):
        for begin, width in ((0, 256), (256, 256), (512, 128)):
            labels = ref[EMB + VECS : EMB + VECS + 16, begin : begin + width].astype(f32)[:1].astype(jnp.int32)
            prepare(ref[:EMB, begin : begin + width], labels, slot + begin // BAND, lhs_ref, rhs_ref)

    def keep_last():
        lhs_ref[:BAND, :] = lhs_ref[CHUNK:, :]
        rhs_ref[:, :BAND] = rhs_ref[:, CHUNK:]

    @pl.when(step == 0)
    def _():
        start_copy.start()
        carry_ref[...] = jnp.zeros_like(carry_ref)
        sum_ref[...] = jnp.zeros_like(sum_ref)
        start_ref[:, :HALO] = low_ref[EMB : EMB + VECS, :]
        start_ref[:, HALO + start_hbm.shape[1] :] = high_ref[EMB : EMB + VECS, :]
        halo(low_ref, CHUNK_BLOCKS + 1 - HALO_BLOCKS)
        pairs(CHUNK_BLOCKS + 1 - HALO_BLOCKS, 0, (HALO_BLOCKS - 1) // 2, True)
        keep_last()

    for j in range(CHUNK // 256):
        here = slice(j * 256, j * 256 + 256)
        prepare(emb_ref[:, here], id_ref[:, here] + 1, 1 + 2 * j, lhs_ref, rhs_ref)
    pairs(0, HALO_BLOCKS - 1 + step * CHUNK_BLOCKS, CHUNK_BLOCKS // 2, True)
    keep_last()

    @pl.when(step == count - 1)
    def _():
        halo(high_ref, 1)
        pairs(0, HALO_BLOCKS - 1 + blocks, (HALO_BLOCKS + 1) // 2, False)
        start_copy.wait()

        def loop(first, number, unroll, one):
            def body(i, carry):
                for u in range(unroll):
                    one(first + i * unroll + u)
                return carry

            lax.fori_loop(0, number // unroll, body, 0)

        def pack0(b):
            here = columns(b * BAND, BAND)
            pack_a[:, here] = (scale_ref[:, here] * start_ref[:, here].astype(f32)).astype(bf16)

        def operate(packed, b):
            product = jnp.dot(packed[:, columns((b - 1) * BAND, 3 * BAND)], weight_ref[b], preferred_element_type=f32)
            return scale_ref[:, columns(b * BAND, BAND)] * product

        def level1(b):
            here = columns(b * BAND, BAND)
            new = operate(pack_a, b) * (1.0 / 0.6) - 0.5 * start_ref[:, here].astype(f32)
            level_a[:, here] = new
            pack_b[:, here] = (scale_ref[:, here] * new).astype(bf16)

        def level2(b):
            here = columns(b * BAND, BAND)
            new = operate(pack_b, b) * (2.0 / 0.6) - level_a[:, here] - start_ref[:, here].astype(f32)
            level_b[:, here] = new
            pack_a[:, here] = (scale_ref[:, here] * new).astype(bf16)

        def level3(b):
            here = columns(b * BAND, BAND)
            new = operate(pack_a, b) * (2.0 / 0.6) - level_b[:, here] - level_a[:, here]
            level_a[:, here] = new
            pack_b[:, here] = (scale_ref[:, here] * new).astype(bf16)

        loop(1, blocks + 8, 20, pack0)
        loop(2, blocks + 6, 18, level1)
        loop(3, blocks + 4, 14, level2)
        loop(3, blocks + 4, 14, level3)
        out_copy = pltpu.make_async_copy(level_a.at[:, HALO : HALO + level_hbm.shape[1]], level_hbm, sems.at[1])
        out_copy.start()

        def grams(i, carry):
            first = HALO_BLOCKS + i * CHUNK_BLOCKS
            image = jnp.concatenate([operate(pack_b, first + u) for u in range(CHUNK_BLOCKS)], axis=1)
            high, low = split(level_a[:, columns(first * BAND, CHUNK)])
            left = jnp.concatenate([high, low], axis=0)
            right = jnp.concatenate([high, low, *split(image)], axis=0)
            sum_ref[...] += lax.dot_general(left, right, (((1,), (1,)), ((), ())), preferred_element_type=f32)
            return carry

        lax.fori_loop(0, count, grams, 0)
        total = sum_ref[:VECS, :] + sum_ref[VECS:, :]
        gram = total[:, :VECS] + total[:, VECS : 2 * VECS]
        image = total[:, 2 * VECS : 3 * VECS] + total[:, 3 * VECS :]
        gram_ref[...] = jnp.concatenate([gram, image], axis=1)
        out_copy.wait()


def filtered(low, high, emb, ids, start):
    rows = emb.shape[1]
    blocks = rows // BAND + 2 * HALO_BLOCKS
    whole = pl.BlockSpec(memory_space=pltpu.VMEM)
    return pl.pallas_call(
        filter_kernel,
        grid=(rows // CHUNK,),
        in_specs=[
            whole,
            whole,
            pl.BlockSpec((EMB, CHUNK), lambda i: (0, i)),
            pl.BlockSpec((1, CHUNK), lambda i: (0, i)),
            pl.BlockSpec(memory_space=pl.ANY),
        ],
        out_specs=[pl.BlockSpec(memory_space=pl.ANY), whole],
        out_shape=[
            jax.ShapeDtypeStruct((VECS, rows), f32),
            jax.ShapeDtypeStruct((VECS, 2 * VECS), f32),
        ],
        scratch_shapes=[
            pltpu.VMEM((CHUNK + BAND, DEPTH), bf16),
            pltpu.VMEM((DEPTH, CHUNK + BAND), bf16),
            pltpu.VMEM((blocks, 3 * BAND, BAND), bf16),
            pltpu.VMEM((1, blocks * BAND), f32),
            pltpu.VMEM((1, BAND), f32),
            pltpu.VMEM((VECS, blocks * BAND), bf16),
            pltpu.VMEM((VECS, blocks * BAND), bf16),
            pltpu.VMEM((VECS, blocks * BAND), bf16),
            pltpu.VMEM((VECS, blocks * BAND), f32),
            pltpu.VMEM((VECS, blocks * BAND), f32),
            pltpu.VMEM((2 * VECS, 4 * VECS), f32),
            pltpu.SemaphoreType.DMA((2,)),
        ],
        compiler_params=pltpu.CompilerParams(vmem_limit_bytes=VMEM_BYTES, dimension_semantics=("arbitrary",)),
        name="filter",
    )(low, high, emb, ids, start)


def basis_kernel(gram_ref, level_ref, basis_ref, ritz_ref, inverse_ref):
    @pl.when(pl.program_id(0) == 0)
    def _():
        row = lax.broadcasted_iota(jnp.int32, (VECS, 2 * VECS), 0)
        col = lax.broadcasted_iota(jnp.int32, (VECS, 2 * VECS), 1)
        work = jnp.where(col < VECS, gram_ref[...], jnp.where(col == row + VECS, 1.0, 0.0))
        for k in range(VECS - 1):
            pivot = work[k : k + 1, :]
            scaled = pivot / jnp.broadcast_to(pivot[:, k : k + 1], pivot.shape)
            factor = jnp.where(row > k, jnp.broadcast_to(work[:, k : k + 1], work.shape), 0.0)
            work = work - factor * scaled
        diagonal = jnp.sum(jnp.where(row == col, work, 0.0), axis=1, keepdims=True)
        inverse = (work * lax.rsqrt(diagonal))[:, VECS:]
        image = gram_ref[:, VECS:]
        exact = lax.Precision.HIGHEST
        left = jnp.dot(inverse, image, precision=exact, preferred_element_type=f32)
        ritz_ref[...] = lax.dot_general(
            left, inverse, (((1,), (1,)), ((), ())), precision=exact, preferred_element_type=f32
        )
        high, low = split(inverse)
        inverse_ref[...] = jnp.concatenate([high, high, low], axis=1)

    high, low = split(level_ref[...])
    basis_ref[...] = jnp.dot(
        inverse_ref[...], jnp.concatenate([high, low, high], axis=0), preferred_element_type=f32
    )


def orthonormal(sums, level):
    rows = level.shape[1]
    whole = pl.BlockSpec(memory_space=pltpu.VMEM)
    return pl.pallas_call(
        basis_kernel,
        grid=(rows // CHUNK,),
        in_specs=[whole, pl.BlockSpec((VECS, CHUNK), lambda i: (0, i))],
        out_specs=[pl.BlockSpec((VECS, CHUNK), lambda i: (0, i)), whole],
        out_shape=[
            jax.ShapeDtypeStruct((VECS, rows), f32),
            jax.ShapeDtypeStruct((VECS, VECS), f32),
        ],
        scratch_shapes=[pltpu.VMEM((VECS, 3 * VECS), bf16)],
        name="basis",
    )(sums, level)


def per_device(embeddings, stream_ids, start_block):
    emb, start = embeddings.T, start_block.T
    rows = emb.shape[1]
    ids = stream_ids.reshape(1, rows)

    def edge(begin):
        here = slice(begin, begin + HALO)
        labels = jnp.broadcast_to((ids[:, here] + 1).astype(bf16), (16, HALO))
        return jnp.concatenate([emb[:, here], start[:, here], labels], axis=0)

    axes = ("ta", "au")
    last = lax.axis_size(axes) - 1
    up = [(i, i + 1) for i in range(last)]
    down = [(i + 1, i) for i in range(last)]
    low = lax.ppermute(edge(rows - HALO), axes, up)
    high = lax.ppermute(edge(0), axes, down)
    level, sums = filtered(low, high, emb, ids, start)
    basis, ritz = orthonormal(lax.psum(sums, axes), level)
    return basis.T, ritz


def solution(mesh):
    placed = (P(("ta", "au"), None), P(("ta", "au")), P(("ta", "au"), None))
    return jax.shard_map(
        per_device,
        mesh=mesh,
        in_specs=placed,
        out_specs=(P(("ta", "au"), None), P()),
        check_vma=False,
    )
```

```python
import jax
import jax.numpy as jnp
from jax import lax
from jax.experimental import pallas as pl
from jax.experimental.pallas import tpu as pltpu
from jax.sharding import PartitionSpec as P

BAND = 128
HALO_BLOCKS = 5
HALO = HALO_BLOCKS * BAND
EMB = 192
VECS = 64
CHUNK_BLOCKS = 16
CHUNK = CHUNK_BLOCKS * BAND
DEPTH = 256
PENALTY = 64.0
EXPONENT = 4.328085122666891
VMEM_BYTES = 62 << 20

bf16 = jnp.bfloat16
f32 = jnp.float32


def columns(start, size):
    return pl.ds(pl.multiple_of(start, BAND), size)


def split(x):
    high = x.astype(bf16)
    return high, (x - high.astype(f32)).astype(bf16)


def prepare(values, labels, slot, lhs_ref, rhs_ref):
    width = values.shape[1]
    values = values.astype(f32)
    normed = (values * lax.rsqrt(jnp.sum(values * values, axis=0, keepdims=True) + 1e-06)).astype(bf16)
    shift = lax.broadcasted_iota(jnp.int32, (16, width), 0)
    bits = (lax.shift_right_logical(jnp.broadcast_to(labels, (16, width)), shift) & 1).astype(f32)
    unset = 1.0 - bits
    first = jnp.where(shift == 0, 1.0, 0.0)
    zeros = jnp.zeros((16, width), bf16)
    rhs = jnp.concatenate(
        [normed, (-PENALTY * unset).astype(bf16), (-PENALTY * bits).astype(bf16), (-first).astype(bf16), zeros], axis=0
    )
    lhs = jnp.concatenate([normed, bits.astype(bf16), unset.astype(bf16), first.astype(bf16), zeros], axis=0)
    rhs_ref[:, slot * BAND : slot * BAND + width] = rhs
    lhs_ref[slot * BAND : slot * BAND + width, :] = lhs.T


def affinity_pair(slot, block, carried, right, lhs_ref, rhs_ref, weight_ref, scale_ref):
    row = lax.broadcasted_iota(jnp.int32, (BAND, BAND), 0)
    col = lax.broadcasted_iota(jnp.int32, (BAND, BAND), 1)
    here = slice(slot * BAND, (slot + 2) * BAND)
    z = jnp.dot(lhs_ref[here, :], rhs_ref[:, here], preferred_element_type=f32)
    e = jnp.exp2(z * EXPONENT)
    own0 = e[:BAND, :BAND].astype(bf16)
    own1 = e[BAND:, BAND:].astype(bf16)
    right0 = jnp.where(row <= col, e[BAND:, :BAND], 0.0).astype(bf16)
    left1 = jnp.where(row >= col, e[:BAND, BAND:], 0.0).astype(bf16)
    weight_ref[block, BAND : 2 * BAND, :] = own0
    weight_ref[block, 2 * BAND :, :] = right0
    weight_ref[block + 1, :BAND, :] = left1
    weight_ref[block + 1, BAND : 2 * BAND, :] = own1
    sum0 = jnp.sum(own0.astype(f32) + right0.astype(f32), axis=0, keepdims=True) + carried
    scale_ref[:, columns(block * BAND, BAND)] = lax.rsqrt(sum0)
    if not right:
        return carried
    z = jnp.dot(
        lhs_ref[(slot + 2) * BAND : (slot + 3) * BAND, :],
        rhs_ref[:, (slot + 1) * BAND : (slot + 2) * BAND],
        preferred_element_type=f32,
    )
    right1 = jnp.where(row <= col, jnp.exp2(z * EXPONENT), 0.0).astype(bf16)
    left2 = right1.T
    weight_ref[block + 1, 2 * BAND :, :] = right1
    weight_ref[block + 2, :BAND, :] = left2
    sum1 = jnp.sum(own1.astype(f32) + left1.astype(f32) + right1.astype(f32), axis=0, keepdims=True)
    scale_ref[:, columns(block * BAND + BAND, BAND)] = lax.rsqrt(sum1)
    return jnp.sum(left2.astype(f32), axis=0, keepdims=True)


def operators(lane, weight_ref, scale_ref, start_ref, pack_a, pack_b, level_a, level_b):
    def at(b):
        return columns(lane(b), BAND)

    def pack0(b):
        pack_a[:, at(b)] = (scale_ref[:, at(b)] * start_ref[:, at(b)].astype(f32)).astype(bf16)

    def operate(packed, b):
        window = packed[:, columns(lane(b - 1), 3 * BAND)]
        return scale_ref[:, at(b)] * jnp.dot(window, weight_ref[b], preferred_element_type=f32)

    def level1(b):
        new = operate(pack_a, b) * (1.0 / 0.6) - 0.5 * start_ref[:, at(b)].astype(f32)
        level_a[:, at(b)] = new
        pack_b[:, at(b)] = (scale_ref[:, at(b)] * new).astype(bf16)

    def level2(b):
        new = operate(pack_b, b) * (2.0 / 0.6) - level_a[:, at(b)] - start_ref[:, at(b)].astype(f32)
        level_b[:, at(b)] = new
        pack_a[:, at(b)] = (scale_ref[:, at(b)] * new).astype(bf16)

    def level3(b):
        new = operate(pack_a, b) * (2.0 / 0.6) - level_b[:, at(b)] - level_a[:, at(b)]
        level_a[:, at(b)] = new
        pack_b[:, at(b)] = (scale_ref[:, at(b)] * new).astype(bf16)

    def products(b, count):
        image = jnp.concatenate([operate(pack_b, b + u) for u in range(count)], axis=1)
        high, low = split(level_a[:, columns(lane(b), count * BAND)])
        left = jnp.concatenate([high, low], axis=0)
        right = jnp.concatenate([high, low, *split(image)], axis=0)
        return lax.dot_general(left, right, (((1,), (1,)), ((), ())), preferred_element_type=f32)

    return pack0, level1, level2, level3, products


def combine(sums):
    total = sums[:VECS, :] + sums[VECS:, :]
    gram = total[:, :VECS] + total[:, VECS : 2 * VECS]
    image = total[:, 2 * VECS : 3 * VECS] + total[:, 3 * VECS :]
    return jnp.concatenate([gram, image], axis=1)


def loop(first, number, unroll, one):
    def body(i, carry):
        for u in range(unroll):
            one(first + i * unroll + u)
        return carry

    lax.fori_loop(0, number // unroll, body, 0)


def unrolled(number, most):
    return max(u for u in range(1, most + 1) if number % u == 0)


def interior_kernel(
    emb_ref, id_ref, start_hbm,
    level_hbm, gram_ref,
    lhs_ref, rhs_ref, weight_ref, scale_ref, carry_ref, start_ref, pack_a, pack_b, level_a, level_b, sum_ref, sems,
):
    step = pl.program_id(0)
    count = pl.num_programs(0)
    own = weight_ref.shape[0] - 2
    start_copy = pltpu.make_async_copy(start_hbm, start_ref.at[:, BAND:], sems.at[0])

    @pl.when(step == 0)
    def _():
        start_copy.start()
        carry_ref[...] = jnp.zeros_like(carry_ref)
        sum_ref[...] = jnp.zeros_like(sum_ref)
        lhs_ref[:BAND, :] = jnp.zeros((BAND, DEPTH), bf16)
        rhs_ref[:, :BAND] = jnp.zeros((DEPTH, BAND), bf16)

    for j in range(CHUNK // 256):
        here = slice(j * 256, j * 256 + 256)
        prepare(emb_ref[:, here], id_ref[:, here] + 1, 1 + 2 * j, lhs_ref, rhs_ref)
    carried = carry_ref[...]
    for i in range(CHUNK_BLOCKS // 2):
        carried = affinity_pair(
            2 * i, step * CHUNK_BLOCKS + 2 * i, carried, True, lhs_ref, rhs_ref, weight_ref, scale_ref
        )
    carry_ref[...] = carried
    lhs_ref[:BAND, :] = lhs_ref[CHUNK:, :]
    rhs_ref[:, :BAND] = rhs_ref[:, CHUNK:]

    @pl.when(step == count - 1)
    def _():
        start_copy.wait()
        pack0, level1, level2, level3, products = operators(
            lambda b: b * BAND, weight_ref, scale_ref, start_ref, pack_a, pack_b, level_a, level_b
        )
        number = own - 2
        loop(2, number, unrolled(number, 20), pack0)
        loop(2, number, unrolled(number, 20), level1)
        loop(2, number, unrolled(number, 20), level2)
        loop(2, number, unrolled(number, 20), level3)
        inner = slice((HALO_BLOCKS + 1) * BAND, (own + 1 - HALO_BLOCKS) * BAND)
        outer = slice(HALO_BLOCKS * BAND, (own - HALO_BLOCKS) * BAND)
        out_copy = pltpu.make_async_copy(level_a.at[:, inner], level_hbm.at[:, outer], sems.at[1])
        out_copy.start()
        number = own - 2 * HALO_BLOCKS
        group = unrolled(number, 16)

        def body(i, carry):
            sum_ref[...] += products(HALO_BLOCKS + 1 + i * group, group)
            return carry

        lax.fori_loop(0, number // group, body, 0)
        gram_ref[...] = combine(sum_ref[...])
        out_copy.wait()


def interior(emb, ids, start):
    rows = emb.shape[1]
    blocks = rows // BAND + 1
    return pl.pallas_call(
        interior_kernel,
        grid=(rows // CHUNK,),
        in_specs=[
            pl.BlockSpec((EMB, CHUNK), lambda i: (0, i)),
            pl.BlockSpec((1, CHUNK), lambda i: (0, i)),
            pl.BlockSpec(memory_space=pl.ANY),
        ],
        out_specs=[pl.BlockSpec(memory_space=pl.ANY), pl.BlockSpec(memory_space=pltpu.VMEM)],
        out_shape=[
            jax.ShapeDtypeStruct((VECS, rows), f32),
            jax.ShapeDtypeStruct((VECS, 2 * VECS), f32),
        ],
        scratch_shapes=[
            pltpu.VMEM((CHUNK + BAND, DEPTH), bf16),
            pltpu.VMEM((DEPTH, CHUNK + BAND), bf16),
            pltpu.VMEM((blocks + 1, 3 * BAND, BAND), bf16),
            pltpu.VMEM((1, blocks * BAND), f32),
            pltpu.VMEM((1, BAND), f32),
            pltpu.VMEM((VECS, blocks * BAND), bf16),
            pltpu.VMEM((VECS, blocks * BAND), bf16),
            pltpu.VMEM((VECS, blocks * BAND), bf16),
            pltpu.VMEM((VECS, blocks * BAND), f32),
            pltpu.VMEM((VECS, blocks * BAND), f32),
            pltpu.VMEM((2 * VECS, 4 * VECS), f32),
            pltpu.SemaphoreType.DMA((2,)),
        ],
        compiler_params=pltpu.CompilerParams(vmem_limit_bytes=VMEM_BYTES, dimension_semantics=("arbitrary",)),
        name="interior",
    )(emb, ids, start)


INSIDE = 2 * HALO
ENDS = 2 * (HALO + INSIDE)
END_BLOCKS = ENDS // BAND


def ends_kernel(
    low_ref, high_ref, id_ref, sums_ref, emb_hbm, start_hbm, level_in,
    level_hbm, gram_ref,
    emb_ref, lhs_ref, rhs_ref, weight_ref, scale_ref, start_ref, pack_a, pack_b, level_a, level_b, sems,
):
    rows = emb_hbm.shape[1]
    first = slice(0, INSIDE)
    last = slice(rows - INSIDE, rows)
    first_at = slice(HALO, HALO + INSIDE)
    last_at = slice(HALO + INSIDE, HALO + 2 * INSIDE)
    copies = [
        pltpu.make_async_copy(source.at[:, there], target.at[:, here], sems.at[i])
        for i, (source, there, target, here) in enumerate(
            (
                (emb_hbm, first, emb_ref, first_at),
                (emb_hbm, last, emb_ref, last_at),
                (start_hbm, first, start_ref, first_at),
                (start_hbm, last, start_ref, last_at),
            )
        )
    ]
    for copy in copies:
        copy.start()
    for ref, begin in ((low_ref, 0), (high_ref, ENDS - HALO)):
        here = slice(begin, begin + HALO)
        emb_ref[:, here] = ref[:EMB, :]
        start_ref[:, here] = ref[EMB : EMB + VECS, :]
    for copy in copies:
        copy.wait()
    for j in range(ENDS // 256):
        here = slice(j * 256, j * 256 + 256)
        prepare(emb_ref[:, here], id_ref[:, here], 2 * j, lhs_ref, rhs_ref)
    carried = jnp.zeros((1, BAND), f32)
    for i in range(END_BLOCKS // 2):
        carried = affinity_pair(
            2 * i, 2 * i, carried, i < END_BLOCKS // 2 - 1, lhs_ref, rhs_ref, weight_ref, scale_ref
        )
    pack0, level1, level2, level3, products = operators(
        lambda b: b * BAND, weight_ref, scale_ref, start_ref, pack_a, pack_b, level_a, level_b
    )
    for margin, one in ((1, pack0), (2, level1), (3, level2), (4, level3)):
        for b in range(margin, END_BLOCKS - margin):
            one(b)
    outs = [
        pltpu.make_async_copy(level_a.at[:, here], level_hbm.at[:, there], sems.at[i])
        for i, (here, there) in enumerate(
            (
                (slice(HALO, 2 * HALO), slice(0, HALO)),
                (slice(ENDS - 2 * HALO, ENDS - HALO), slice(rows - HALO, rows)),
            )
        )
    ]
    for copy in outs:
        copy.start()
    sums = products(HALO_BLOCKS, HALO_BLOCKS) + products(END_BLOCKS - 2 * HALO_BLOCKS, HALO_BLOCKS)
    gram_ref[...] = sums_ref[...] + combine(sums)
    for copy in outs:
        copy.wait()


def ends(low, high, ids, sums, emb, start, level):
    whole = pl.BlockSpec(memory_space=pltpu.VMEM)
    away = pl.BlockSpec(memory_space=pl.ANY)
    return pl.pallas_call(
        ends_kernel,
        in_specs=[whole, whole, whole, whole, away, away, away],
        out_specs=[away, whole],
        out_shape=[
            jax.ShapeDtypeStruct(level.shape, f32),
            jax.ShapeDtypeStruct((VECS, 2 * VECS), f32),
        ],
        input_output_aliases={6: 0},
        scratch_shapes=[
            pltpu.VMEM((EMB, ENDS), bf16),
            pltpu.VMEM((ENDS, DEPTH), bf16),
            pltpu.VMEM((DEPTH, ENDS), bf16),
            pltpu.VMEM((END_BLOCKS, 3 * BAND, BAND), bf16),
            pltpu.VMEM((1, ENDS), f32),
            pltpu.VMEM((VECS, ENDS), bf16),
            pltpu.VMEM((VECS, ENDS), bf16),
            pltpu.VMEM((VECS, ENDS), bf16),
            pltpu.VMEM((VECS, ENDS), f32),
            pltpu.VMEM((VECS, ENDS), f32),
            pltpu.SemaphoreType.DMA((4,)),
        ],
        compiler_params=pltpu.CompilerParams(vmem_limit_bytes=VMEM_BYTES),
        name="ends",
    )(low, high, ids, sums, emb, start, level)


def total(x, axes):
    for axis in axes:
        size = lax.axis_size(axis)
        if size & (size - 1):
            x = lax.psum(x, axis)
            continue
        stride = 1
        while stride < size:
            x = x + lax.ppermute(x, axis, [(i, i ^ stride) for i in range(size)])
            stride *= 2
    return x


def basis_kernel(gram_ref, level_ref, basis_ref, ritz_ref, inverse_ref):
    @pl.when(pl.program_id(0) == 0)
    def _():
        row = lax.broadcasted_iota(jnp.int32, (VECS, 2 * VECS), 0)
        col = lax.broadcasted_iota(jnp.int32, (VECS, 2 * VECS), 1)
        work = jnp.where(col < VECS, gram_ref[...], jnp.where(col == row + VECS, 1.0, 0.0))
        for k in range(VECS - 1):
            pivot = work[k : k + 1, :]
            scaled = pivot / jnp.broadcast_to(pivot[:, k : k + 1], pivot.shape)
            factor = jnp.where(row > k, jnp.broadcast_to(work[:, k : k + 1], work.shape), 0.0)
            work = work - factor * scaled
        diagonal = jnp.sum(jnp.where(row == col, work, 0.0), axis=1, keepdims=True)
        inverse = (work * lax.rsqrt(diagonal))[:, VECS:]
        image = gram_ref[:, VECS:]
        exact = lax.Precision.HIGHEST
        left = jnp.dot(inverse, image, precision=exact, preferred_element_type=f32)
        ritz_ref[...] = lax.dot_general(
            left, inverse, (((1,), (1,)), ((), ())), precision=exact, preferred_element_type=f32
        )
        high, low = split(inverse)
        inverse_ref[...] = jnp.concatenate([high, high, low], axis=1)

    high, low = split(level_ref[...])
    basis_ref[...] = jnp.dot(
        inverse_ref[...], jnp.concatenate([high, low, high], axis=0), preferred_element_type=f32
    )


def orthonormal(sums, level):
    rows = level.shape[1]
    whole = pl.BlockSpec(memory_space=pltpu.VMEM)
    return pl.pallas_call(
        basis_kernel,
        grid=(rows // CHUNK,),
        in_specs=[whole, pl.BlockSpec((VECS, CHUNK), lambda i: (0, i))],
        out_specs=[pl.BlockSpec((VECS, CHUNK), lambda i: (0, i)), whole],
        out_shape=[
            jax.ShapeDtypeStruct((VECS, rows), f32),
            jax.ShapeDtypeStruct((VECS, VECS), f32),
        ],
        scratch_shapes=[pltpu.VMEM((VECS, 3 * VECS), bf16)],
        name="basis",
    )(sums, level)


def per_device(embeddings, stream_ids, start_block):
    emb, start = embeddings.T, start_block.T
    rows = emb.shape[1]
    ids = stream_ids.reshape(1, rows)

    def edge(begin):
        here = slice(begin, begin + HALO)
        labels = jnp.broadcast_to((ids[:, here] + 1).astype(bf16), (16, HALO))
        return jnp.concatenate([emb[:, here], start[:, here], labels], axis=0)

    axes = ("ta", "au")
    last = lax.axis_size(axes) - 1
    up = [(i, i + 1) for i in range(last)]
    down = [(i + 1, i) for i in range(last)]
    low = lax.ppermute(edge(rows - HALO), axes, up)
    high = lax.ppermute(edge(0), axes, down)
    level, sums = interior(emb, ids, start)
    labels = jnp.concatenate(
        [
            low[EMB + VECS : EMB + VECS + 1, :].astype(jnp.int32),
            ids[:, :INSIDE] + 1,
            ids[:, rows - INSIDE :] + 1,
            high[EMB + VECS : EMB + VECS + 1, :].astype(jnp.int32),
        ],
        axis=1,
    )
    level, sums = ends(low, high, labels, sums, emb, start, level)
    basis, ritz = orthonormal(total(sums, axes), level)
    return basis.T, ritz


def solution(mesh):
    placed = (P(("ta", "au"), None), P(("ta", "au")), P(("ta", "au"), None))
    return jax.shard_map(
        per_device,
        mesh=mesh,
        in_specs=placed,
        out_specs=(P(("ta", "au"), None), P()),
        check_vma=False,
    )
```

```python
import jax
import jax.numpy as jnp
from jax import lax
from jax.experimental import pallas as pl
from jax.experimental.pallas import tpu as pltpu
from jax.sharding import PartitionSpec as P

BAND = 128
HALO_BLOCKS = 5
HALO = HALO_BLOCKS * BAND
EMB = 192
VECS = 64
CHUNK_BLOCKS = 16
CHUNK = CHUNK_BLOCKS * BAND
DEPTH = 256
PENALTY = 64.0
EXPONENT = 4.328085122666891
VMEM_BYTES = 62 << 20

bf16 = jnp.bfloat16
f32 = jnp.float32


def columns(start, size):
    return pl.ds(pl.multiple_of(start, BAND), size)


def split(x):
    high = x.astype(bf16)
    return high, (x - high.astype(f32)).astype(bf16)


def prepare(values, labels, slot, lhs_ref, rhs_ref):
    width = values.shape[1]
    values = values.astype(f32)
    normed = (values * lax.rsqrt(jnp.sum(values * values, axis=0, keepdims=True) + 1e-06)).astype(bf16)
    shift = lax.broadcasted_iota(jnp.int32, (16, width), 0)
    bits = (lax.shift_right_logical(jnp.broadcast_to(labels, (16, width)), shift) & 1).astype(f32)
    unset = 1.0 - bits
    first = jnp.where(shift == 0, 1.0, 0.0)
    zeros = jnp.zeros((16, width), bf16)
    rhs = jnp.concatenate(
        [normed, (-PENALTY * unset).astype(bf16), (-PENALTY * bits).astype(bf16), (-first).astype(bf16), zeros], axis=0
    )
    lhs = jnp.concatenate([normed, bits.astype(bf16), unset.astype(bf16), first.astype(bf16), zeros], axis=0)
    rhs_ref[:, slot * BAND : slot * BAND + width] = rhs
    lhs_ref[:, slot * BAND : slot * BAND + width] = lhs


def affinity_pair(slot, block, carried, right, lhs_ref, rhs_ref, weight_ref, scale_ref):
    row = lax.broadcasted_iota(jnp.int32, (BAND, BAND), 0)
    col = lax.broadcasted_iota(jnp.int32, (BAND, BAND), 1)
    here = slice(slot * BAND, (slot + 2) * BAND)
    z = lax.dot_general(lhs_ref[:, here], rhs_ref[:, here], (((0,), (0,)), ((), ())), preferred_element_type=f32)
    e = jnp.exp2(z * EXPONENT)
    own0 = e[:BAND, :BAND].astype(bf16)
    own1 = e[BAND:, BAND:].astype(bf16)
    right0 = jnp.where(row <= col, e[BAND:, :BAND], 0.0).astype(bf16)
    left1 = jnp.where(row >= col, e[:BAND, BAND:], 0.0).astype(bf16)
    weight_ref[block, BAND : 2 * BAND, :] = own0
    weight_ref[block, 2 * BAND :, :] = right0
    weight_ref[block + 1, :BAND, :] = left1
    weight_ref[block + 1, BAND : 2 * BAND, :] = own1
    sum0 = jnp.sum(own0.astype(f32) + right0.astype(f32), axis=0, keepdims=True) + carried
    scale_ref[:, columns(block * BAND, BAND)] = lax.rsqrt(sum0)
    if not right:
        return carried
    z = lax.dot_general(
        lhs_ref[:, (slot + 2) * BAND : (slot + 3) * BAND],
        rhs_ref[:, (slot + 1) * BAND : (slot + 2) * BAND],
        (((0,), (0,)), ((), ())),
        preferred_element_type=f32,
    )
    right1 = jnp.where(row <= col, jnp.exp2(z * EXPONENT), 0.0).astype(bf16)
    left2 = right1.T
    weight_ref[block + 1, 2 * BAND :, :] = right1
    weight_ref[block + 2, :BAND, :] = left2
    sum1 = jnp.sum(own1.astype(f32) + left1.astype(f32) + right1.astype(f32), axis=0, keepdims=True)
    scale_ref[:, columns(block * BAND + BAND, BAND)] = lax.rsqrt(sum1)
    return jnp.sum(left2.astype(f32), axis=0, keepdims=True)


def operators(lane, weight_ref, scale_ref, start_ref, pack_a, pack_b, level_a, level_b):
    def at(b):
        return columns(lane(b), BAND)

    def pack0(b):
        pack_a[:, at(b)] = (scale_ref[:, at(b)] * start_ref[:, at(b)].astype(f32)).astype(bf16)

    def operate(packed, b):
        window = packed[:, columns(lane(b - 1), 3 * BAND)]
        return scale_ref[:, at(b)] * jnp.dot(window, weight_ref[b], preferred_element_type=f32)

    def level1(b):
        new = operate(pack_a, b) * (1.0 / 0.6) - 0.5 * start_ref[:, at(b)].astype(f32)
        level_a[:, at(b)] = new
        pack_b[:, at(b)] = (scale_ref[:, at(b)] * new).astype(bf16)

    def level2(b):
        new = operate(pack_b, b) * (2.0 / 0.6) - level_a[:, at(b)] - start_ref[:, at(b)].astype(f32)
        level_b[:, at(b)] = new
        pack_a[:, at(b)] = (scale_ref[:, at(b)] * new).astype(bf16)

    def level3(b):
        new = operate(pack_a, b) * (2.0 / 0.6) - level_b[:, at(b)] - level_a[:, at(b)]
        level_a[:, at(b)] = new
        pack_b[:, at(b)] = (scale_ref[:, at(b)] * new).astype(bf16)

    def products(b, count):
        image = jnp.concatenate([operate(pack_b, b + u) for u in range(count)], axis=1)
        high, low = split(level_a[:, columns(lane(b), count * BAND)])
        left = jnp.concatenate([high, *split(image)], axis=0)
        right = jnp.concatenate([high, low], axis=0)
        return lax.dot_general(left, right, (((1,), (1,)), ((), ())), preferred_element_type=f32)

    return pack0, level1, level2, level3, products


def combine(sums):
    cross = sums[:VECS, VECS:]
    gram = sums[:VECS, :VECS] + cross + cross.T
    image = sums[VECS : 2 * VECS, :] + sums[2 * VECS :, :]
    image = (image[:, :VECS] + image[:, VECS:]).T
    return jnp.concatenate([gram, image], axis=1)


def loop(first, number, unroll, one):
    def body(i, carry):
        for u in range(unroll):
            one(first + i * unroll + u)
        return carry

    lax.fori_loop(0, number // unroll, body, 0)


def unrolled(number, most):
    return max(u for u in range(1, most + 1) if number % u == 0)


def interior_kernel(
    emb_ref, id_ref, chunk_ref,
    level_hbm, gram_ref,
    lhs_ref, rhs_ref, weight_ref, scale_ref, carry_ref, start_ref, pack_a, pack_b, level_a, level_b, sum_ref, sems,
):
    step = pl.program_id(0)
    count = pl.num_programs(0)
    own = weight_ref.shape[0] - 2
    @pl.when(step == 0)
    def _():
        carry_ref[...] = jnp.zeros_like(carry_ref)
        sum_ref[...] = jnp.zeros_like(sum_ref)
        lhs_ref[:, :BAND] = jnp.zeros((DEPTH, BAND), bf16)
        rhs_ref[:, :BAND] = jnp.zeros((DEPTH, BAND), bf16)

    start_ref[:, columns(step * CHUNK + BAND, CHUNK)] = chunk_ref[...]
    for j in range(CHUNK // 256):
        here = slice(j * 256, j * 256 + 256)
        prepare(emb_ref[:, here], id_ref[:, here] + 1, 1 + 2 * j, lhs_ref, rhs_ref)
    carried = carry_ref[...]
    for i in range(CHUNK_BLOCKS // 2):
        carried = affinity_pair(
            2 * i, step * CHUNK_BLOCKS + 2 * i, carried, True, lhs_ref, rhs_ref, weight_ref, scale_ref
        )
    carry_ref[...] = carried
    lhs_ref[:, :BAND] = lhs_ref[:, CHUNK:]
    rhs_ref[:, :BAND] = rhs_ref[:, CHUNK:]

    @pl.when(step == count - 1)
    def _():
        pack0, level1, level2, level3, products = operators(
            lambda b: b * BAND, weight_ref, scale_ref, start_ref, pack_a, pack_b, level_a, level_b
        )
        number = own - 2
        loop(2, number, unrolled(number, 100), pack0)
        loop(2, number, unrolled(number, 100), level1)
        loop(2, number, unrolled(number, 100), level2)
        loop(2, number, unrolled(number, 100), level3)
        inner = slice((HALO_BLOCKS + 1) * BAND, (own + 1 - HALO_BLOCKS) * BAND)
        outer = slice(HALO_BLOCKS * BAND, (own - HALO_BLOCKS) * BAND)
        out_copy = pltpu.make_async_copy(level_a.at[:, inner], level_hbm.at[:, outer], sems)
        out_copy.start()
        number = own - 2 * HALO_BLOCKS
        group = unrolled(number, 26)

        def body(i, carry):
            sum_ref[...] += products(HALO_BLOCKS + 1 + i * group, group)
            return carry

        lax.fori_loop(0, number // group, body, 0)
        gram_ref[...] = combine(sum_ref[...])
        out_copy.wait()


def interior(emb, ids, start):
    rows = emb.shape[1]
    blocks = rows // BAND + 1
    return pl.pallas_call(
        interior_kernel,
        grid=(rows // CHUNK,),
        in_specs=[
            pl.BlockSpec((EMB, CHUNK), lambda i: (0, i)),
            pl.BlockSpec((1, CHUNK), lambda i: (0, i)),
            pl.BlockSpec((VECS, CHUNK), lambda i: (0, i)),
        ],
        out_specs=[pl.BlockSpec(memory_space=pl.ANY), pl.BlockSpec(memory_space=pltpu.VMEM)],
        out_shape=[
            jax.ShapeDtypeStruct((VECS, rows), f32),
            jax.ShapeDtypeStruct((VECS, 2 * VECS), f32),
        ],
        scratch_shapes=[
            pltpu.VMEM((DEPTH, CHUNK + BAND), bf16),
            pltpu.VMEM((DEPTH, CHUNK + BAND), bf16),
            pltpu.VMEM((blocks + 1, 3 * BAND, BAND), bf16),
            pltpu.VMEM((1, blocks * BAND), f32),
            pltpu.VMEM((1, BAND), f32),
            pltpu.VMEM((VECS, blocks * BAND), bf16),
            pltpu.VMEM((VECS, blocks * BAND), bf16),
            pltpu.VMEM((VECS, blocks * BAND), bf16),
            pltpu.VMEM((VECS, blocks * BAND), f32),
            pltpu.VMEM((VECS, blocks * BAND), f32),
            pltpu.VMEM((3 * VECS, 2 * VECS), f32),
            pltpu.SemaphoreType.DMA,
        ],
        compiler_params=pltpu.CompilerParams(vmem_limit_bytes=VMEM_BYTES, dimension_semantics=("arbitrary",)),
        name="interior",
    )(emb, ids, start)


INSIDE = 2 * HALO
ENDS = 2 * (HALO + INSIDE)
END_BLOCKS = ENDS // BAND


def ends_kernel(
    low_ref, high_ref, id_ref, sums_ref, emb_hbm, start_hbm, level_in,
    level_hbm, gram_ref,
    emb_ref, lhs_ref, rhs_ref, weight_ref, scale_ref, start_ref, pack_a, pack_b, level_a, level_b, sems,
):
    rows = emb_hbm.shape[1]
    first = slice(0, INSIDE)
    last = slice(rows - INSIDE, rows)
    first_at = slice(HALO, HALO + INSIDE)
    last_at = slice(HALO + INSIDE, HALO + 2 * INSIDE)
    copies = [
        pltpu.make_async_copy(source.at[:, there], target.at[:, here], sems.at[i])
        for i, (source, there, target, here) in enumerate(
            (
                (emb_hbm, first, emb_ref, first_at),
                (emb_hbm, last, emb_ref, last_at),
                (start_hbm, first, start_ref, first_at),
                (start_hbm, last, start_ref, last_at),
            )
        )
    ]
    for copy in copies:
        copy.start()
    for ref, begin in ((low_ref, 0), (high_ref, ENDS - HALO)):
        here = slice(begin, begin + HALO)
        emb_ref[:, here] = ref[:EMB, :]
        start_ref[:, here] = ref[EMB : EMB + VECS, :]
    for copy in copies:
        copy.wait()
    for j in range(ENDS // 256):
        here = slice(j * 256, j * 256 + 256)
        prepare(emb_ref[:, here], id_ref[:, here], 2 * j, lhs_ref, rhs_ref)
    carried = jnp.zeros((1, BAND), f32)
    for i in range(END_BLOCKS // 2):
        carried = affinity_pair(
            2 * i, 2 * i, carried, i < END_BLOCKS // 2 - 1, lhs_ref, rhs_ref, weight_ref, scale_ref
        )
    pack0, level1, level2, level3, products = operators(
        lambda b: b * BAND, weight_ref, scale_ref, start_ref, pack_a, pack_b, level_a, level_b
    )
    for margin, one in ((1, pack0), (2, level1), (3, level2), (4, level3)):
        for b in range(margin, END_BLOCKS - margin):
            one(b)
    outs = [
        pltpu.make_async_copy(level_a.at[:, here], level_hbm.at[:, there], sems.at[i])
        for i, (here, there) in enumerate(
            (
                (slice(HALO, 2 * HALO), slice(0, HALO)),
                (slice(ENDS - 2 * HALO, ENDS - HALO), slice(rows - HALO, rows)),
            )
        )
    ]
    for copy in outs:
        copy.start()
    sums = products(HALO_BLOCKS, HALO_BLOCKS) + products(END_BLOCKS - 2 * HALO_BLOCKS, HALO_BLOCKS)
    gram_ref[...] = sums_ref[...] + combine(sums)
    for copy in outs:
        copy.wait()


def ends(low, high, ids, sums, emb, start, level):
    whole = pl.BlockSpec(memory_space=pltpu.VMEM)
    away = pl.BlockSpec(memory_space=pl.ANY)
    return pl.pallas_call(
        ends_kernel,
        in_specs=[whole, whole, whole, whole, away, away, away],
        out_specs=[away, whole],
        out_shape=[
            jax.ShapeDtypeStruct(level.shape, f32),
            jax.ShapeDtypeStruct((VECS, 2 * VECS), f32),
        ],
        input_output_aliases={6: 0},
        scratch_shapes=[
            pltpu.VMEM((EMB, ENDS), bf16),
            pltpu.VMEM((DEPTH, ENDS), bf16),
            pltpu.VMEM((DEPTH, ENDS), bf16),
            pltpu.VMEM((END_BLOCKS, 3 * BAND, BAND), bf16),
            pltpu.VMEM((1, ENDS), f32),
            pltpu.VMEM((VECS, ENDS), bf16),
            pltpu.VMEM((VECS, ENDS), bf16),
            pltpu.VMEM((VECS, ENDS), bf16),
            pltpu.VMEM((VECS, ENDS), f32),
            pltpu.VMEM((VECS, ENDS), f32),
            pltpu.SemaphoreType.DMA((4,)),
        ],
        compiler_params=pltpu.CompilerParams(vmem_limit_bytes=VMEM_BYTES),
        name="ends",
    )(low, high, ids, sums, emb, start, level)


def total(x, axes):
    for axis in axes:
        size = lax.axis_size(axis)
        if size & (size - 1):
            x = lax.psum(x, axis)
            continue
        stride = 1
        while stride < size:
            x = x + lax.ppermute(x, axis, [(i, i ^ stride) for i in range(size)])
            stride *= 2
    return x


def basis_kernel(gram_ref, level_hbm, basis_ref, ritz_ref, inverse_ref, level_ref, sem):
    width = basis_ref.shape[1]

    @pl.when(pl.program_id(0) == 0)
    def _():
        copy = pltpu.make_async_copy(level_hbm, level_ref, sem)
        copy.start()
        row = lax.broadcasted_iota(jnp.int32, (VECS, 2 * VECS), 0)
        col = lax.broadcasted_iota(jnp.int32, (VECS, 2 * VECS), 1)
        work = jnp.where(col < VECS, gram_ref[...], jnp.where(col == row + VECS, 1.0, 0.0))
        for k in range(VECS - 1):
            pivot = work[k : k + 1, :]
            scaled = pivot / jnp.broadcast_to(pivot[:, k : k + 1], pivot.shape)
            factor = jnp.where(row > k, jnp.broadcast_to(work[:, k : k + 1], work.shape), 0.0)
            work = work - factor * scaled
        diagonal = jnp.sum(jnp.where(row == col, work, 0.0), axis=1, keepdims=True)
        inverse = (work * lax.rsqrt(diagonal))[:, VECS:]
        image = gram_ref[:, VECS:]
        exact = lax.Precision.HIGHEST
        left = jnp.dot(inverse, image, precision=exact, preferred_element_type=f32)
        ritz_ref[...] = lax.dot_general(
            left, inverse, (((1,), (1,)), ((), ())), precision=exact, preferred_element_type=f32
        )
        high, low = split(inverse)
        inverse_ref[...] = jnp.concatenate([high, high, low], axis=1)
        copy.wait()

    high, low = split(level_ref[:, columns(pl.program_id(0) * width, width)])
    basis_ref[...] = jnp.dot(
        inverse_ref[...], jnp.concatenate([high, low, high], axis=0), preferred_element_type=f32
    )


def orthonormal(sums, level):
    rows = level.shape[1]
    width = 4 * CHUNK
    whole = pl.BlockSpec(memory_space=pltpu.VMEM)
    return pl.pallas_call(
        basis_kernel,
        grid=(rows // width,),
        in_specs=[whole, pl.BlockSpec(memory_space=pl.ANY)],
        out_specs=[pl.BlockSpec((VECS, width), lambda i: (0, i)), whole],
        out_shape=[
            jax.ShapeDtypeStruct((VECS, rows), f32),
            jax.ShapeDtypeStruct((VECS, VECS), f32),
        ],
        scratch_shapes=[
            pltpu.VMEM((VECS, 3 * VECS), bf16),
            pltpu.VMEM((VECS, rows), f32),
            pltpu.SemaphoreType.DMA,
        ],
        compiler_params=pltpu.CompilerParams(vmem_limit_bytes=VMEM_BYTES),
        name="basis",
    )(sums, level)


def per_device(embeddings, stream_ids, start_block):
    emb, start = embeddings.T, start_block.T
    rows = emb.shape[1]
    ids = stream_ids.reshape(1, rows)

    def edge(begin):
        here = slice(begin, begin + HALO)
        labels = jnp.broadcast_to((ids[:, here] + 1).astype(bf16), (16, HALO))
        return jnp.concatenate([emb[:, here], start[:, here], labels], axis=0)

    axes = ("ta", "au")
    last = lax.axis_size(axes) - 1
    up = [(i, i + 1) for i in range(last)]
    down = [(i + 1, i) for i in range(last)]
    low = lax.ppermute(edge(rows - HALO), axes, up)
    high = lax.ppermute(edge(0), axes, down)
    level, sums = interior(emb, ids, start)
    labels = jnp.concatenate(
        [
            low[EMB + VECS : EMB + VECS + 1, :].astype(jnp.int32),
            ids[:, :INSIDE] + 1,
            ids[:, rows - INSIDE :] + 1,
            high[EMB + VECS : EMB + VECS + 1, :].astype(jnp.int32),
        ],
        axis=1,
    )
    level, sums = ends(low, high, labels, sums, emb, start, level)
    basis, ritz = orthonormal(total(sums, axes), level)
    return basis.T, ritz


def solution(mesh):
    placed = (P(("ta", "au"), None), P(("ta", "au")), P(("ta", "au"), None))
    return jax.shard_map(
        per_device,
        mesh=mesh,
        in_specs=placed,
        out_specs=(P(("ta", "au"), None), P()),
        check_vma=False,
    )
```

```python
import jax
import jax.numpy as jnp
from jax import lax
from jax.experimental import pallas as pl
from jax.experimental.pallas import tpu as pltpu
from jax.sharding import PartitionSpec as P

BAND = 128
HALO_BLOCKS = 5
HALO = HALO_BLOCKS * BAND
EMB = 192
VECS = 64
CHUNK_BLOCKS = 32
CHUNK = CHUNK_BLOCKS * BAND
DEPTH = 256
PENALTY = 64.0
GROUP = 8
EXPONENT = 4.328085122666891
VMEM_BYTES = 62 << 20

bf16 = jnp.bfloat16
f32 = jnp.float32


def columns(start, size):
    return pl.ds(pl.multiple_of(start, BAND), size)


def split(x):
    high = x.astype(bf16)
    return high, (x - high.astype(f32)).astype(bf16)


def prepare(values, labels, slot, lhs_ref, rhs_ref):
    width = values.shape[1]
    values = values.astype(f32)
    normed = (values * lax.rsqrt(jnp.sum(values * values, axis=0, keepdims=True) + 1e-06)).astype(bf16)
    shift = lax.broadcasted_iota(jnp.int32, (16, width), 0)
    bits = (lax.shift_right_logical(jnp.broadcast_to(labels, (16, width)), shift) & 1).astype(f32)
    unset = 1.0 - bits
    first = jnp.where(shift == 0, 1.0, 0.0)
    zeros = jnp.zeros((16, width), bf16)
    rhs = jnp.concatenate(
        [normed, (-PENALTY * unset).astype(bf16), (-PENALTY * bits).astype(bf16), (-first).astype(bf16), zeros], axis=0
    )
    lhs = jnp.concatenate([normed, bits.astype(bf16), unset.astype(bf16), first.astype(bf16), zeros], axis=0)
    rhs_ref[:, slot * BAND : slot * BAND + width] = rhs
    lhs_ref[:, slot * BAND : slot * BAND + width] = lhs


def affinity_pair(slot, block, carried, right, lhs_ref, rhs_ref, weight_ref, scale_ref):
    row = lax.broadcasted_iota(jnp.int32, (BAND, BAND), 0)
    col = lax.broadcasted_iota(jnp.int32, (BAND, BAND), 1)
    for i in range(2):
        here = slice((slot + i) * BAND, (slot + i + 1) * BAND)
        both = right or i == 0
        there = slice((slot + i) * BAND, (slot + i + 1 + both) * BAND)
        z = lax.dot_general(lhs_ref[:, there], rhs_ref[:, here], (((0,), (0,)), ((), ())), preferred_element_type=f32)
        e = jnp.exp2(z * EXPONENT)
        own = e[:BAND].astype(bf16)
        weight_ref[block + i, BAND : 2 * BAND, :] = own
        if not both:
            return carried
        after = jnp.where(row <= col, e[BAND:], 0.0).astype(bf16)
        before = after.T
        weight_ref[block + i, 2 * BAND :, :] = after
        weight_ref[block + i + 1, :BAND, :] = before
        degree = jnp.sum(own.astype(f32) + after.astype(f32), axis=0, keepdims=True) + carried
        scale_ref[:, columns((block + i) * BAND, BAND)] = lax.rsqrt(degree)
        carried = jnp.sum(before.astype(f32), axis=0, keepdims=True)
    return carried


def operators(lane, weight_ref, scale_ref, start_ref, pack_a, pack_b, level_a, level_b):
    def at(b):
        return columns(lane(b), BAND)

    def pack0(b):
        pack_a[:, at(b)] = (scale_ref[:, at(b)] * start_ref[:, at(b)].astype(f32)).astype(bf16)

    def operate(packed, b):
        window = packed[:, columns(lane(b - 1), 3 * BAND)]
        return scale_ref[:, at(b)] * jnp.dot(window, weight_ref[b], preferred_element_type=f32)

    def level1(b):
        new = operate(pack_a, b) * (1.0 / 0.6) - 0.5 * start_ref[:, at(b)].astype(f32)
        level_a[:, at(b)] = new
        pack_b[:, at(b)] = (scale_ref[:, at(b)] * new).astype(bf16)

    def level2(b):
        new = operate(pack_b, b) * (2.0 / 0.6) - level_a[:, at(b)] - start_ref[:, at(b)].astype(f32)
        level_b[:, at(b)] = new
        pack_a[:, at(b)] = (scale_ref[:, at(b)] * new).astype(bf16)

    def level3(b):
        new = operate(pack_a, b) * (2.0 / 0.6) - level_b[:, at(b)] - level_a[:, at(b)]
        level_a[:, at(b)] = new
        pack_b[:, at(b)] = (scale_ref[:, at(b)] * new).astype(bf16)

    def products(b, count):
        image = jnp.concatenate([operate(pack_b, b + u) for u in range(count)], axis=1)
        high, low = split(level_a[:, columns(lane(b), count * BAND)])
        left = jnp.concatenate([high, *split(image)], axis=0)
        right = jnp.concatenate([high, low], axis=0)
        return lax.dot_general(left, right, (((1,), (1,)), ((), ())), preferred_element_type=f32)

    return pack0, level1, level2, level3, products


def combine(sums):
    cross = sums[:VECS, VECS:]
    gram = sums[:VECS, :VECS] + cross + cross.T
    image = sums[VECS : 2 * VECS, :] + sums[2 * VECS :, :]
    image = (image[:, :VECS] + image[:, VECS:]).T
    return jnp.concatenate([gram, image], axis=1)


def loop(first, number, unroll, one):
    def body(i, carry):
        for u in range(unroll):
            one(first + i * unroll + u)
        return carry

    lax.fori_loop(0, number // unroll, body, 0)


def unrolled(number, most):
    return max(u for u in range(1, most + 1) if number % u == 0)


def interior_kernel(
    emb_ref, id_ref, chunk_ref,
    level_hbm, gram_ref,
    lhs_ref, rhs_ref, weight_ref, scale_ref, carry_ref, start_ref, pack_a, pack_b, level_a, level_b, sum_ref, sems,
):
    step = pl.program_id(0)
    count = pl.num_programs(0)
    own = weight_ref.shape[0] - 2
    @pl.when(step == 0)
    def _():
        carry_ref[...] = jnp.zeros_like(carry_ref)
        sum_ref[...] = jnp.zeros_like(sum_ref)
        lhs_ref[:, :BAND] = jnp.zeros((DEPTH, BAND), bf16)
        rhs_ref[:, :BAND] = jnp.zeros((DEPTH, BAND), bf16)

    start_ref[:, columns(step * CHUNK + BAND, CHUNK)] = chunk_ref[...]
    for j in range(CHUNK // 256):
        here = slice(j * 256, j * 256 + 256)
        prepare(emb_ref[:, here], id_ref[:, here] + 1, 1 + 2 * j, lhs_ref, rhs_ref)
    carried = carry_ref[...]
    for i in range(CHUNK_BLOCKS // 2):
        carried = affinity_pair(
            2 * i, step * CHUNK_BLOCKS + 2 * i, carried, True, lhs_ref, rhs_ref, weight_ref, scale_ref
        )
    carry_ref[...] = carried
    lhs_ref[:, :BAND] = lhs_ref[:, CHUNK:]
    rhs_ref[:, :BAND] = rhs_ref[:, CHUNK:]

    @pl.when(step == count - 1)
    def _():
        pack0, level1, level2, level3, products = operators(
            lambda b: b * BAND, weight_ref, scale_ref, start_ref, pack_a, pack_b, level_a, level_b
        )
        number = own - 2
        loop(2, number, unrolled(number, 100), pack0)
        loop(2, number, unrolled(number, 100), level1)
        loop(2, number, unrolled(number, 100), level2)
        loop(2, number, unrolled(number, 100), level3)
        inner = slice((HALO_BLOCKS + 1) * BAND, (own + 1 - HALO_BLOCKS) * BAND)
        outer = slice(HALO_BLOCKS * BAND, (own - HALO_BLOCKS) * BAND)
        out_copy = pltpu.make_async_copy(level_a.at[:, inner], level_hbm.at[:, outer], sems)
        out_copy.start()
        number = own - 2 * HALO_BLOCKS
        group = unrolled(number, 26)

        def body(i, carry):
            sum_ref[...] += products(HALO_BLOCKS + 1 + i * group, group)
            return carry

        lax.fori_loop(0, number // group, body, 0)
        gram_ref[...] = combine(sum_ref[...])
        out_copy.wait()


def interior(emb, ids, start):
    rows = emb.shape[1]
    blocks = rows // BAND + 1
    return pl.pallas_call(
        interior_kernel,
        grid=(rows // CHUNK,),
        in_specs=[
            pl.BlockSpec((EMB, CHUNK), lambda i: (0, i)),
            pl.BlockSpec((1, CHUNK), lambda i: (0, i)),
            pl.BlockSpec((VECS, CHUNK), lambda i: (0, i)),
        ],
        out_specs=[pl.BlockSpec(memory_space=pl.ANY), pl.BlockSpec(memory_space=pltpu.VMEM)],
        out_shape=[
            jax.ShapeDtypeStruct((VECS, rows), f32),
            jax.ShapeDtypeStruct((VECS, 2 * VECS), f32),
        ],
        scratch_shapes=[
            pltpu.VMEM((DEPTH, CHUNK + BAND), bf16),
            pltpu.VMEM((DEPTH, CHUNK + BAND), bf16),
            pltpu.VMEM((blocks + 1, 3 * BAND, BAND), bf16),
            pltpu.VMEM((1, blocks * BAND), f32),
            pltpu.VMEM((1, BAND), f32),
            pltpu.VMEM((VECS, blocks * BAND), bf16),
            pltpu.VMEM((VECS, blocks * BAND), bf16),
            pltpu.VMEM((VECS, blocks * BAND), bf16),
            pltpu.VMEM((VECS, blocks * BAND), f32),
            pltpu.VMEM((VECS, blocks * BAND), f32),
            pltpu.VMEM((3 * VECS, 2 * VECS), f32),
            pltpu.SemaphoreType.DMA,
        ],
        compiler_params=pltpu.CompilerParams(vmem_limit_bytes=VMEM_BYTES, dimension_semantics=("arbitrary",)),
        name="interior",
    )(emb, ids, start)


def edges_kernel(emb_hbm, id_hbm, start_hbm, first_ref, last_ref, label_ref, sems):
    rows = emb_hbm.shape[1]
    copies = []
    for side, (target, begin) in enumerate(((first_ref, 0), (last_ref, rows - HALO))):
        there = slice(begin, begin + HALO)
        copies += [
            pltpu.make_async_copy(id_hbm.at[:, there], label_ref.at[side], sems.at[side, 0]),
            pltpu.make_async_copy(emb_hbm.at[:, there], target.at[:EMB, :], sems.at[side, 1]),
            pltpu.make_async_copy(start_hbm.at[:, there], target.at[EMB : EMB + VECS, :], sems.at[side, 2]),
        ]
    for copy in copies:
        copy.start()
    for side, target in enumerate((first_ref, last_ref)):
        copies[3 * side].wait()
        labels = jnp.broadcast_to(label_ref[side] + 1, (16, HALO)).astype(f32)
        target[EMB + VECS :, :] = labels.astype(bf16)
        copies[3 * side + 1].wait()
        copies[3 * side + 2].wait()


def edges(emb, ids, start):
    whole = pl.BlockSpec(memory_space=pltpu.VMEM)
    away = pl.BlockSpec(memory_space=pl.ANY)
    return pl.pallas_call(
        edges_kernel,
        in_specs=[away, away, away],
        out_specs=[whole, whole],
        out_shape=[jax.ShapeDtypeStruct((EMB + VECS + 16, HALO), bf16)] * 2,
        scratch_shapes=[pltpu.VMEM((2, 1, HALO), jnp.int32), pltpu.SemaphoreType.DMA((2, 3))],
        compiler_params=pltpu.CompilerParams(vmem_limit_bytes=VMEM_BYTES),
        name="edges",
    )(emb, ids, start)


INSIDE = 2 * HALO
ENDS = 2 * (HALO + INSIDE)
END_BLOCKS = ENDS // BAND


def ends_kernel(
    low_ref, high_ref, sums_ref, id_hbm, emb_hbm, start_hbm, level_in,
    level_hbm, gram_ref,
    id_ref, emb_ref, lhs_ref, rhs_ref, weight_ref, scale_ref, start_ref, pack_a, pack_b, level_a, level_b, sems,
):
    rows = emb_hbm.shape[1]
    first = slice(0, INSIDE)
    last = slice(rows - INSIDE, rows)
    first_at = slice(HALO, HALO + INSIDE)
    last_at = slice(HALO + INSIDE, HALO + 2 * INSIDE)
    copies = [
        pltpu.make_async_copy(source.at[:, there], target.at[:, here], sems.at[i])
        for i, (source, there, target, here) in enumerate(
            (
                (id_hbm, first, id_ref, first_at),
                (id_hbm, last, id_ref, last_at),
                (emb_hbm, first, emb_ref, first_at),
                (emb_hbm, last, emb_ref, last_at),
                (start_hbm, first, start_ref, first_at),
                (start_hbm, last, start_ref, last_at),
            )
        )
    ]
    for copy in copies:
        copy.start()
    for ref, begin in ((low_ref, 0), (high_ref, ENDS - HALO)):
        here = slice(begin, begin + HALO)
        emb_ref[:, here] = ref[:EMB, :]
        start_ref[:, here] = ref[EMB : EMB + VECS, :]
        id_ref[:, here] = ref[EMB + VECS :, :].astype(f32)[:1].astype(jnp.int32) - 1
    for copy in copies:
        copy.wait()
    for j in range(ENDS // 256):
        here = slice(j * 256, j * 256 + 256)
        prepare(emb_ref[:, here], id_ref[:, here] + 1, 2 * j, lhs_ref, rhs_ref)
    carried = jnp.zeros((1, BAND), f32)
    for i in range(END_BLOCKS // 2):
        carried = affinity_pair(
            2 * i, 2 * i, carried, i < END_BLOCKS // 2 - 1, lhs_ref, rhs_ref, weight_ref, scale_ref
        )
    pack0, level1, level2, level3, products = operators(
        lambda b: b * BAND, weight_ref, scale_ref, start_ref, pack_a, pack_b, level_a, level_b
    )
    for margin, one in ((1, pack0), (2, level1), (3, level2), (4, level3)):
        for b in range(margin, END_BLOCKS - margin):
            one(b)
    outs = [
        pltpu.make_async_copy(level_a.at[:, here], level_hbm.at[:, there], sems.at[i])
        for i, (here, there) in enumerate(
            (
                (slice(HALO, 2 * HALO), slice(0, HALO)),
                (slice(ENDS - 2 * HALO, ENDS - HALO), slice(rows - HALO, rows)),
            )
        )
    ]
    for copy in outs:
        copy.start()
    sums = products(HALO_BLOCKS, HALO_BLOCKS) + products(END_BLOCKS - 2 * HALO_BLOCKS, HALO_BLOCKS)
    gram_ref[...] = sums_ref[...] + combine(sums)
    for copy in outs:
        copy.wait()


def ends(low, high, ids, sums, emb, start, level):
    whole = pl.BlockSpec(memory_space=pltpu.VMEM)
    away = pl.BlockSpec(memory_space=pl.ANY)
    return pl.pallas_call(
        ends_kernel,
        in_specs=[whole, whole, whole, away, away, away, away],
        out_specs=[away, whole],
        out_shape=[
            jax.ShapeDtypeStruct(level.shape, f32),
            jax.ShapeDtypeStruct((VECS, 2 * VECS), f32),
        ],
        input_output_aliases={6: 0},
        scratch_shapes=[
            pltpu.VMEM((1, ENDS), jnp.int32),
            pltpu.VMEM((EMB, ENDS), bf16),
            pltpu.VMEM((DEPTH, ENDS), bf16),
            pltpu.VMEM((DEPTH, ENDS), bf16),
            pltpu.VMEM((END_BLOCKS, 3 * BAND, BAND), bf16),
            pltpu.VMEM((1, ENDS), f32),
            pltpu.VMEM((VECS, ENDS), bf16),
            pltpu.VMEM((VECS, ENDS), bf16),
            pltpu.VMEM((VECS, ENDS), bf16),
            pltpu.VMEM((VECS, ENDS), f32),
            pltpu.VMEM((VECS, ENDS), f32),
            pltpu.SemaphoreType.DMA((6,)),
        ],
        compiler_params=pltpu.CompilerParams(vmem_limit_bytes=VMEM_BYTES),
        name="ends",
    )(low, high, sums, ids, emb, start, level)


def total(x, axes):
    for axis in axes:
        size = lax.axis_size(axis)
        if size & (size - 1):
            x = lax.psum(x, axis)
            continue
        stride = 1
        while stride < size:
            x = x + lax.ppermute(x, axis, [(i, i ^ stride) for i in range(size)])
            stride *= 2
    return x


def basis_kernel(gram_ref, level_hbm, basis_ref, ritz_ref, inverse_ref, level_ref, sem):
    width = basis_ref.shape[1]

    @pl.when(pl.program_id(0) == 0)
    def _():
        copy = pltpu.make_async_copy(level_hbm, level_ref, sem)
        copy.start()
        row = lax.broadcasted_iota(jnp.int32, (VECS, 2 * VECS), 0)
        col = lax.broadcasted_iota(jnp.int32, (VECS, 2 * VECS), 1)
        work = jnp.where(col < VECS, gram_ref[...], jnp.where(col == row + VECS, 1.0, 0.0))
        for k in range(0, VECS, GROUP):
            spread = [jnp.broadcast_to(work[:, j : j + 1], work.shape) for j in range(k, k + GROUP)]
            pivots = [work[j : j + 1, :] for j in range(k, k + GROUP)]
            for j in range(GROUP):
                factor = jnp.where(row > k + j, spread[j] * (1.0 / spread[j][k + j : k + j + 1, :]), 0.0)
                for m in range(j + 1, GROUP):
                    spread[m] = spread[m] - factor * spread[m][k + j : k + j + 1, :]
                    pivots[m] = pivots[m] - factor[k + m : k + m + 1, :] * pivots[j]
                work = work - factor * pivots[j]
        diagonal = jnp.sum(jnp.where(row == col, work, 0.0), axis=1, keepdims=True)
        inverse = (work * lax.rsqrt(diagonal))[:, VECS:]
        image = gram_ref[:, VECS:]
        exact = lax.Precision.HIGHEST
        left = jnp.dot(inverse, image, precision=exact, preferred_element_type=f32)
        ritz_ref[...] = lax.dot_general(
            left, inverse, (((1,), (1,)), ((), ())), precision=exact, preferred_element_type=f32
        )
        high, low = split(inverse)
        inverse_ref[...] = jnp.concatenate([high, high, low], axis=1)
        copy.wait()

    high, low = split(level_ref[:, columns(pl.program_id(0) * width, width)])
    basis_ref[...] = jnp.dot(
        inverse_ref[...], jnp.concatenate([high, low, high], axis=0), preferred_element_type=f32
    )


def orthonormal(sums, level):
    rows = level.shape[1]
    width = 2 * CHUNK
    whole = pl.BlockSpec(memory_space=pltpu.VMEM)
    return pl.pallas_call(
        basis_kernel,
        grid=(rows // width,),
        in_specs=[whole, pl.BlockSpec(memory_space=pl.ANY)],
        out_specs=[pl.BlockSpec((VECS, width), lambda i: (0, i)), whole],
        out_shape=[
            jax.ShapeDtypeStruct((VECS, rows), f32),
            jax.ShapeDtypeStruct((VECS, VECS), f32),
        ],
        scratch_shapes=[
            pltpu.VMEM((VECS, 3 * VECS), bf16),
            pltpu.VMEM((VECS, rows), f32),
            pltpu.SemaphoreType.DMA,
        ],
        compiler_params=pltpu.CompilerParams(vmem_limit_bytes=VMEM_BYTES),
        name="basis",
    )(sums, level)


def per_device(embeddings, stream_ids, start_block):
    emb, start = embeddings.T, start_block.T
    rows = emb.shape[1]
    ids = stream_ids.reshape(1, rows)

    first, last = edges(emb, ids, start)
    axes = ("ta", "au")
    steps = range(lax.axis_size(axes) - 1)
    low = lax.ppermute(last, axes, [(i, i + 1) for i in steps])
    high = lax.ppermute(first, axes, [(i + 1, i) for i in steps])
    level, sums = interior(emb, ids, start)
    level, sums = ends(low, high, ids, sums, emb, start, level)
    basis, ritz = orthonormal(total(sums, axes), level)
    return basis.T, ritz


def solution(mesh):
    placed = (P(("ta", "au"), None), P(("ta", "au")), P(("ta", "au"), None))
    return jax.shard_map(
        per_device,
        mesh=mesh,
        in_specs=placed,
        out_specs=(P(("ta", "au"), None), P()),
        check_vma=False,
    )
```

```python
import jax
import jax.numpy as jnp
from jax import lax
from jax.experimental import pallas as pl
from jax.experimental.pallas import tpu as pltpu
from jax.sharding import PartitionSpec as P

BAND = 128
HALO_BLOCKS = 5
HALO = HALO_BLOCKS * BAND
EMB = 192
VECS = 64
CHUNK_BLOCKS = 32
CHUNK = CHUNK_BLOCKS * BAND
DEPTH = 256
PENALTY = 64.0
GROUP = 8
GRAM_BLOCKS = 26
EXPONENT = 4.328085122666891
VMEM_BYTES = 62 << 20

bf16 = jnp.bfloat16
f32 = jnp.float32


def columns(start, size):
    if isinstance(start, int):
        return slice(start, start + size)
    return pl.ds(pl.multiple_of(start, BAND), size)


def split(x):
    high = x.astype(bf16)
    return high, (x - high.astype(f32)).astype(bf16)


def prepare(values, labels, slot, lhs_ref, rhs_ref):
    width = values.shape[1]
    values = values.astype(f32)
    normed = (values * lax.rsqrt(jnp.sum(values * values, axis=0, keepdims=True) + 1e-06)).astype(bf16)
    shift = lax.broadcasted_iota(jnp.int32, (16, width), 0)
    bits = (lax.shift_right_logical(jnp.broadcast_to(labels, (16, width)), shift) & 1).astype(f32)
    unset = 1.0 - bits
    first = jnp.where(shift == 0, 1.0, 0.0)
    zeros = jnp.zeros((16, width), bf16)
    rhs = jnp.concatenate(
        [normed, (-PENALTY * unset).astype(bf16), (-PENALTY * bits).astype(bf16), (-first).astype(bf16), zeros], axis=0
    )
    lhs = jnp.concatenate([normed, bits.astype(bf16), unset.astype(bf16), first.astype(bf16), zeros], axis=0)
    rhs_ref[:, slot * BAND : slot * BAND + width] = rhs
    lhs_ref[:, slot * BAND : slot * BAND + width] = lhs


def affinity_pair(slot, block, carried, right, lhs_ref, rhs_ref, weight_ref, scale_ref):
    row = lax.broadcasted_iota(jnp.int32, (BAND, BAND), 0)
    col = lax.broadcasted_iota(jnp.int32, (BAND, BAND), 1)
    for i in range(2):
        here = slice((slot + i) * BAND, (slot + i + 1) * BAND)
        both = right or i == 0
        there = slice((slot + i) * BAND, (slot + i + 1 + both) * BAND)
        z = lax.dot_general(lhs_ref[:, there], rhs_ref[:, here], (((0,), (0,)), ((), ())), preferred_element_type=f32)
        e = jnp.exp2(z * EXPONENT)
        own = e[:BAND].astype(bf16)
        weight_ref[block + i, BAND : 2 * BAND, :] = own
        if not both:
            return carried
        after = jnp.where(row <= col, e[BAND:], 0.0).astype(bf16)
        before = after.T
        weight_ref[block + i, 2 * BAND :, :] = after
        weight_ref[block + i + 1, :BAND, :] = before
        degree = jnp.sum(own.astype(f32) + after.astype(f32), axis=0, keepdims=True) + carried
        scale_ref[:, columns((block + i) * BAND, BAND)] = lax.rsqrt(degree)
        carried = jnp.sum(before.astype(f32), axis=0, keepdims=True)
    return carried


def operators(lane, weight_ref, scale_ref, start_ref, pack_a, pack_b, level_a, level_b):
    def at(b):
        return columns(lane(b), BAND)

    def pack0(b):
        pack_a[:, at(b)] = (scale_ref[:, at(b)] * start_ref[:, at(b)].astype(f32)).astype(bf16)

    def operate(packed, b):
        window = packed[:, columns(lane(b - 1), 3 * BAND)]
        return scale_ref[:, at(b)] * jnp.dot(window, weight_ref[b], preferred_element_type=f32)

    def level1(b):
        new = operate(pack_a, b) * (1.0 / 0.6) - 0.5 * start_ref[:, at(b)].astype(f32)
        level_a[:, at(b)] = new
        pack_b[:, at(b)] = (scale_ref[:, at(b)] * new).astype(bf16)

    def level2(b):
        new = operate(pack_b, b) * (2.0 / 0.6) - level_a[:, at(b)] - start_ref[:, at(b)].astype(f32)
        level_b[:, at(b)] = new
        pack_a[:, at(b)] = (scale_ref[:, at(b)] * new).astype(bf16)

    def level3(b):
        new = operate(pack_a, b) * (2.0 / 0.6) - level_b[:, at(b)] - level_a[:, at(b)]
        level_a[:, at(b)] = new
        pack_b[:, at(b)] = (scale_ref[:, at(b)] * new).astype(bf16)

    def products(b, count):
        image = jnp.concatenate([operate(pack_b, b + u) for u in range(count)], axis=1)
        high, low = split(level_a[:, columns(lane(b), count * BAND)])
        left = jnp.concatenate([high, *split(image)], axis=0)
        right = jnp.concatenate([high, low], axis=0)
        return lax.dot_general(left, right, (((1,), (1,)), ((), ())), preferred_element_type=f32)

    return pack0, level1, level2, level3, products


def combine(sums):
    cross = sums[:VECS, VECS:]
    gram = sums[:VECS, :VECS] + cross + cross.T
    image = sums[VECS : 2 * VECS, :] + sums[2 * VECS :, :]
    image = (image[:, :VECS] + image[:, VECS:]).T
    return jnp.concatenate([gram, image], axis=1)


def interior_kernel(
    emb_ref, id_ref, chunk_ref,
    level_hbm, gram_ref,
    lhs_ref, rhs_ref, weight_ref, scale_ref, carry_ref, start_ref, pack_a, pack_b, level_a, level_b, sems,
):
    step = pl.program_id(0)
    count = pl.num_programs(0)
    own = weight_ref.shape[0] - 2
    @pl.when(step == 0)
    def _():
        carry_ref[...] = jnp.zeros_like(carry_ref)
        lhs_ref[:, :BAND] = jnp.zeros((DEPTH, BAND), bf16)
        rhs_ref[:, :BAND] = jnp.zeros((DEPTH, BAND), bf16)

    start_ref[:, columns(step * CHUNK + BAND, CHUNK)] = chunk_ref[...]
    for j in range(CHUNK // 256):
        here = slice(j * 256, j * 256 + 256)
        prepare(emb_ref[:, here], id_ref[:, here] + 1, 1 + 2 * j, lhs_ref, rhs_ref)
    carried = carry_ref[...]
    for i in range(CHUNK_BLOCKS // 2):
        carried = affinity_pair(
            2 * i, step * CHUNK_BLOCKS + 2 * i, carried, True, lhs_ref, rhs_ref, weight_ref, scale_ref
        )
    carry_ref[...] = carried
    lhs_ref[:, :BAND] = lhs_ref[:, CHUNK:]
    rhs_ref[:, :BAND] = rhs_ref[:, CHUNK:]

    @pl.when(step == count - 1)
    def _():
        pack0, level1, level2, level3, products = operators(
            lambda b: b * BAND, weight_ref, scale_ref, start_ref, pack_a, pack_b, level_a, level_b
        )
        for one in (pack0, level1, level2, level3):
            for b in range(2, own):
                one(b)
        inner = slice((HALO_BLOCKS + 1) * BAND, (own + 1 - HALO_BLOCKS) * BAND)
        outer = slice(HALO_BLOCKS * BAND, (own - HALO_BLOCKS) * BAND)
        out_copy = pltpu.make_async_copy(level_a.at[:, inner], level_hbm.at[:, outer], sems)
        out_copy.start()
        sums = jnp.zeros((3 * VECS, 2 * VECS), f32)
        for b in range(HALO_BLOCKS + 1, own + 1 - HALO_BLOCKS, GRAM_BLOCKS):
            sums += products(b, min(GRAM_BLOCKS, own + 1 - HALO_BLOCKS - b))
        gram_ref[...] = combine(sums)
        out_copy.wait()


def interior(emb, ids, start):
    rows = emb.shape[1]
    blocks = rows // BAND + 1
    return pl.pallas_call(
        interior_kernel,
        grid=(rows // CHUNK,),
        in_specs=[
            pl.BlockSpec((EMB, CHUNK), lambda i: (0, i)),
            pl.BlockSpec((1, CHUNK), lambda i: (0, i)),
            pl.BlockSpec((VECS, CHUNK), lambda i: (0, i)),
        ],
        out_specs=[pl.BlockSpec(memory_space=pl.ANY), pl.BlockSpec(memory_space=pltpu.VMEM)],
        out_shape=[
            jax.ShapeDtypeStruct((VECS, rows), f32),
            jax.ShapeDtypeStruct((VECS, 2 * VECS), f32),
        ],
        scratch_shapes=[
            pltpu.VMEM((DEPTH, CHUNK + BAND), bf16),
            pltpu.VMEM((DEPTH, CHUNK + BAND), bf16),
            pltpu.VMEM((blocks + 1, 3 * BAND, BAND), bf16),
            pltpu.VMEM((1, blocks * BAND), f32),
            pltpu.VMEM((1, BAND), f32),
            pltpu.VMEM((VECS, blocks * BAND), bf16),
            pltpu.VMEM((VECS, blocks * BAND), bf16),
            pltpu.VMEM((VECS, blocks * BAND), bf16),
            pltpu.VMEM((VECS, blocks * BAND), f32),
            pltpu.VMEM((VECS, blocks * BAND), f32),
            pltpu.SemaphoreType.DMA,
        ],
        compiler_params=pltpu.CompilerParams(vmem_limit_bytes=VMEM_BYTES, dimension_semantics=("arbitrary",)),
        name="interior",
    )(emb, ids, start)


def edges_kernel(emb_hbm, id_hbm, start_hbm, first_ref, last_ref, label_ref, row_ref, sems):
    rows = emb_hbm.shape[1]
    copies = []
    for side, (target, begin) in enumerate(((first_ref, 0), (last_ref, rows - HALO))):
        there = slice(begin, begin + HALO)
        copies += [
            pltpu.make_async_copy(id_hbm.at[:, there], label_ref.at[side], sems.at[side, 0]),
            pltpu.make_async_copy(emb_hbm.at[:, there], target.at[:EMB, :], sems.at[side, 1]),
            pltpu.make_async_copy(start_hbm.at[:, there], target.at[EMB : EMB + VECS, :], sems.at[side, 2]),
        ]
    for copy in copies:
        copy.start()
    rows = []
    for side, target in enumerate((first_ref, last_ref)):
        copies[3 * side].wait()
        labels = jnp.broadcast_to(label_ref[side] + 1, (16, HALO)).astype(f32)
        row_ref[side] = labels.astype(bf16)
        rows.append(pltpu.make_async_copy(row_ref.at[side], target.at[EMB + VECS :, :], sems.at[side, 3]))
        rows[side].start()
    for side in range(2):
        copies[3 * side + 1].wait()
        copies[3 * side + 2].wait()
        rows[side].wait()


def edges(emb, ids, start):
    away = pl.BlockSpec(memory_space=pl.ANY)
    return pl.pallas_call(
        edges_kernel,
        in_specs=[away, away, away],
        out_specs=[away, away],
        out_shape=[jax.ShapeDtypeStruct((EMB + VECS + 16, HALO), bf16)] * 2,
        scratch_shapes=[
            pltpu.VMEM((2, 1, HALO), jnp.int32),
            pltpu.VMEM((2, 16, HALO), bf16),
            pltpu.SemaphoreType.DMA((2, 4)),
        ],
        compiler_params=pltpu.CompilerParams(vmem_limit_bytes=VMEM_BYTES),
        name="edges",
    )(emb, ids, start)


INSIDE = 2 * HALO
ENDS = 2 * (HALO + INSIDE)
END_BLOCKS = ENDS // BAND


def ends_kernel(
    low_ref, high_ref, sums_ref, id_hbm, emb_hbm, start_hbm, level_in,
    level_hbm, gram_ref,
    id_ref, emb_ref, lhs_ref, rhs_ref, weight_ref, scale_ref, start_ref, pack_a, pack_b, level_a, level_b, sems,
):
    rows = emb_hbm.shape[1]
    first = slice(0, INSIDE)
    last = slice(rows - INSIDE, rows)
    first_at = slice(HALO, HALO + INSIDE)
    last_at = slice(HALO + INSIDE, HALO + 2 * INSIDE)
    copies = [
        pltpu.make_async_copy(source.at[:, there], target.at[:, here], sems.at[i])
        for i, (source, there, target, here) in enumerate(
            (
                (id_hbm, first, id_ref, first_at),
                (id_hbm, last, id_ref, last_at),
                (emb_hbm, first, emb_ref, first_at),
                (emb_hbm, last, emb_ref, last_at),
                (start_hbm, first, start_ref, first_at),
                (start_hbm, last, start_ref, last_at),
            )
        )
    ]
    for copy in copies:
        copy.start()
    for ref, begin in ((low_ref, 0), (high_ref, ENDS - HALO)):
        here = slice(begin, begin + HALO)
        emb_ref[:, here] = ref[:EMB, :]
        start_ref[:, here] = ref[EMB : EMB + VECS, :]
        id_ref[:, here] = ref[EMB + VECS :, :].astype(f32)[:1].astype(jnp.int32) - 1
    for copy in copies[:4]:
        copy.wait()
    for j in range(ENDS // 256):
        here = slice(j * 256, j * 256 + 256)
        prepare(emb_ref[:, here], id_ref[:, here] + 1, 2 * j, lhs_ref, rhs_ref)
    carried = jnp.zeros((1, BAND), f32)
    for i in range(END_BLOCKS // 2):
        carried = affinity_pair(
            2 * i, 2 * i, carried, i < END_BLOCKS // 2 - 1, lhs_ref, rhs_ref, weight_ref, scale_ref
        )
    pack0, level1, level2, level3, products = operators(
        lambda b: b * BAND, weight_ref, scale_ref, start_ref, pack_a, pack_b, level_a, level_b
    )
    half = END_BLOCKS // 2
    for copy in copies[4:]:
        copy.wait()
    for margin, one in ((1, pack0), (2, level1), (3, level2), (4, level3)):
        for b in (*range(margin, half - margin), *range(half + margin, END_BLOCKS - margin)):
            one(b)
    outs = [
        pltpu.make_async_copy(level_a.at[:, here], level_hbm.at[:, there], sems.at[i])
        for i, (here, there) in enumerate(
            (
                (slice(HALO, 2 * HALO), slice(0, HALO)),
                (slice(ENDS - 2 * HALO, ENDS - HALO), slice(rows - HALO, rows)),
            )
        )
    ]
    for copy in outs:
        copy.start()
    sums = products(HALO_BLOCKS, HALO_BLOCKS) + products(END_BLOCKS - 2 * HALO_BLOCKS, HALO_BLOCKS)
    gram_ref[...] = sums_ref[...] + combine(sums)
    for copy in outs:
        copy.wait()


def ends(low, high, ids, sums, emb, start, level):
    whole = pl.BlockSpec(memory_space=pltpu.VMEM)
    away = pl.BlockSpec(memory_space=pl.ANY)
    return pl.pallas_call(
        ends_kernel,
        in_specs=[whole, whole, whole, away, away, away, away],
        out_specs=[away, whole],
        out_shape=[
            jax.ShapeDtypeStruct(level.shape, f32),
            jax.ShapeDtypeStruct((VECS, 2 * VECS), f32),
        ],
        input_output_aliases={6: 0},
        scratch_shapes=[
            pltpu.VMEM((1, ENDS), jnp.int32),
            pltpu.VMEM((EMB, ENDS), bf16),
            pltpu.VMEM((DEPTH, ENDS), bf16),
            pltpu.VMEM((DEPTH, ENDS), bf16),
            pltpu.VMEM((END_BLOCKS, 3 * BAND, BAND), bf16),
            pltpu.VMEM((1, ENDS), f32),
            pltpu.VMEM((VECS, ENDS), bf16),
            pltpu.VMEM((VECS, ENDS), bf16),
            pltpu.VMEM((VECS, ENDS), bf16),
            pltpu.VMEM((VECS, ENDS), f32),
            pltpu.VMEM((VECS, ENDS), f32),
            pltpu.SemaphoreType.DMA((6,)),
        ],
        compiler_params=pltpu.CompilerParams(vmem_limit_bytes=VMEM_BYTES),
        name="ends",
    )(low, high, sums, ids, emb, start, level)


def total(x, axes):
    for axis in axes:
        size = lax.axis_size(axis)
        if size & (size - 1):
            x = lax.psum(x, axis)
            continue
        stride = 1
        while stride < size:
            x = x + lax.ppermute(x, axis, [(i, i ^ stride) for i in range(size)])
            stride *= 2
    return x


def basis_kernel(gram_ref, level_hbm, basis_ref, ritz_ref, inverse_ref, level_ref, sem):
    width = basis_ref.shape[1]

    @pl.when(pl.program_id(0) == 0)
    def _():
        copy = pltpu.make_async_copy(level_hbm, level_ref, sem)
        copy.start()
        row = lax.broadcasted_iota(jnp.int32, (VECS, 2 * VECS), 0)
        col = lax.broadcasted_iota(jnp.int32, (VECS, 2 * VECS), 1)
        work = jnp.where(col < VECS, gram_ref[...], jnp.where(col == row + VECS, 1.0, 0.0))
        for k in range(0, VECS, GROUP):
            spread = [jnp.broadcast_to(work[:, j : j + 1], work.shape) for j in range(k, k + GROUP)]
            pivots = [work[j : j + 1, :] for j in range(k, k + GROUP)]
            for j in range(GROUP):
                factor = jnp.where(row > k + j, spread[j] * (1.0 / spread[j][k + j : k + j + 1, :]), 0.0)
                for m in range(j + 1, GROUP):
                    spread[m] = spread[m] - factor * spread[m][k + j : k + j + 1, :]
                    pivots[m] = pivots[m] - factor[k + m : k + m + 1, :] * pivots[j]
                work = work - factor * pivots[j]
        diagonal = jnp.sum(jnp.where(row == col, work, 0.0), axis=1, keepdims=True)
        inverse = (work * lax.rsqrt(diagonal))[:, VECS:]
        image = gram_ref[:, VECS:]
        exact = lax.Precision.HIGHEST
        left = jnp.dot(inverse, image, precision=exact, preferred_element_type=f32)
        ritz_ref[...] = lax.dot_general(
            left, inverse, (((1,), (1,)), ((), ())), precision=exact, preferred_element_type=f32
        )
        high, low = split(inverse)
        inverse_ref[...] = jnp.concatenate([high, high, low], axis=1)
        copy.wait()

    high, low = split(level_ref[:, columns(pl.program_id(0) * width, width)])
    basis_ref[...] = jnp.dot(
        inverse_ref[...], jnp.concatenate([high, low, high], axis=0), preferred_element_type=f32
    )


def orthonormal(sums, level):
    rows = level.shape[1]
    width = 2 * CHUNK
    whole = pl.BlockSpec(memory_space=pltpu.VMEM)
    return pl.pallas_call(
        basis_kernel,
        grid=(rows // width,),
        in_specs=[whole, pl.BlockSpec(memory_space=pl.ANY)],
        out_specs=[pl.BlockSpec((VECS, width), lambda i: (0, i)), whole],
        out_shape=[
            jax.ShapeDtypeStruct((VECS, rows), f32),
            jax.ShapeDtypeStruct((VECS, VECS), f32),
        ],
        scratch_shapes=[
            pltpu.VMEM((VECS, 3 * VECS), bf16),
            pltpu.VMEM((VECS, rows), f32),
            pltpu.SemaphoreType.DMA,
        ],
        compiler_params=pltpu.CompilerParams(vmem_limit_bytes=VMEM_BYTES),
        name="basis",
    )(sums, level)


def per_device(embeddings, stream_ids, start_block):
    emb, start = embeddings.T, start_block.T
    rows = emb.shape[1]
    ids = stream_ids.reshape(1, rows)

    first, last = edges(emb, ids, start)
    axes = ("ta", "au")
    steps = range(lax.axis_size(axes) - 1)
    low = lax.ppermute(last, axes, [(i, i + 1) for i in steps])
    high = lax.ppermute(first, axes, [(i + 1, i) for i in steps])
    level, sums = interior(emb, ids, start)
    level, sums = ends(low, high, ids, sums, emb, start, level)
    basis, ritz = orthonormal(total(sums, axes), level)
    return basis.T, ritz


def solution(mesh):
    placed = (P(("ta", "au"), None), P(("ta", "au")), P(("ta", "au"), None))
    return jax.shard_map(
        per_device,
        mesh=mesh,
        in_specs=placed,
        out_specs=(P(("ta", "au"), None), P()),
        check_vma=False,
    )
```

```python
import jax
import jax.numpy as jnp
from jax import lax
from jax.experimental import pallas as pl
from jax.experimental.pallas import tpu as pltpu
from jax.sharding import PartitionSpec as P

BAND = 128
HALO_BLOCKS = 5
HALO = HALO_BLOCKS * BAND
EMB = 192
VECS = 64
CHUNK_BLOCKS = 32
CHUNK = CHUNK_BLOCKS * BAND
DEPTH = 256
PENALTY = 64.0
GROUP = 8
GRAM_BLOCKS = 26
EXPONENT = 4.328085122666891
VMEM_BYTES = 62 << 20

bf16 = jnp.bfloat16
f32 = jnp.float32


def columns(start, size):
    if isinstance(start, int):
        return slice(start, start + size)
    return pl.ds(pl.multiple_of(start, BAND), size)


def split(x):
    high = x.astype(bf16)
    return high, (x - high.astype(f32)).astype(bf16)


def prepare(values, labels, slot, lhs_ref, rhs_ref):
    width = values.shape[1]
    values = values.astype(f32)
    normed = (values * lax.rsqrt(jnp.sum(values * values, axis=0, keepdims=True) + 1e-06)).astype(bf16)
    shift = lax.broadcasted_iota(jnp.int32, (16, width), 0)
    bits = (lax.shift_right_logical(jnp.broadcast_to(labels, (16, width)), shift) & 1).astype(f32)
    unset = 1.0 - bits
    first = jnp.where(shift == 0, 1.0, 0.0)
    zeros = jnp.zeros((16, width), bf16)
    rhs = jnp.concatenate(
        [normed, (-PENALTY * unset).astype(bf16), (-PENALTY * bits).astype(bf16), (-first).astype(bf16), zeros], axis=0
    )
    lhs = jnp.concatenate([normed, bits.astype(bf16), unset.astype(bf16), first.astype(bf16), zeros], axis=0)
    rhs_ref[:, slot * BAND : slot * BAND + width] = rhs
    lhs_ref[:, slot * BAND : slot * BAND + width] = lhs


def affinity_pair(slot, block, carried, right, lhs_ref, rhs_ref, weight_ref, scale_ref):
    row = lax.broadcasted_iota(jnp.int32, (BAND, BAND), 0)
    col = lax.broadcasted_iota(jnp.int32, (BAND, BAND), 1)
    for i in range(2):
        here = slice((slot + i) * BAND, (slot + i + 1) * BAND)
        both = right or i == 0
        there = slice((slot + i) * BAND, (slot + i + 1 + both) * BAND)
        z = lax.dot_general(lhs_ref[:, there], rhs_ref[:, here], (((0,), (0,)), ((), ())), preferred_element_type=f32)
        e = jnp.exp2(z * EXPONENT)
        own = e[:BAND].astype(bf16)
        weight_ref[block + i, BAND : 2 * BAND, :] = own
        if not both:
            return carried
        after = jnp.where(row <= col, e[BAND:], 0.0).astype(bf16)
        before = after.T
        weight_ref[block + i, 2 * BAND :, :] = after
        weight_ref[block + i + 1, :BAND, :] = before
        degree = jnp.sum(own.astype(f32) + after.astype(f32), axis=0, keepdims=True) + carried
        scale_ref[:, columns((block + i) * BAND, BAND)] = lax.rsqrt(degree)
        carried = jnp.sum(before.astype(f32), axis=0, keepdims=True)
    return carried


def operators(lane, weight_ref, scale_ref, start_ref, pack_a, pack_b, level_a, level_b):
    def at(b):
        return columns(lane(b), BAND)

    def pack0(b):
        pack_a[:, at(b)] = (scale_ref[:, at(b)] * start_ref[:, at(b)].astype(f32)).astype(bf16)

    def operate(packed, b):
        window = packed[:, columns(lane(b - 1), 3 * BAND)]
        return scale_ref[:, at(b)] * jnp.dot(window, weight_ref[b], preferred_element_type=f32)

    def level1(b):
        new = operate(pack_a, b) * (1.0 / 0.6) - 0.5 * start_ref[:, at(b)].astype(f32)
        level_a[:, at(b)] = new
        pack_b[:, at(b)] = (scale_ref[:, at(b)] * new).astype(bf16)

    def level2(b):
        new = operate(pack_b, b) * (2.0 / 0.6) - level_a[:, at(b)] - start_ref[:, at(b)].astype(f32)
        level_b[:, at(b)] = new
        pack_a[:, at(b)] = (scale_ref[:, at(b)] * new).astype(bf16)

    def level3(b):
        new = operate(pack_a, b) * (2.0 / 0.6) - level_b[:, at(b)] - level_a[:, at(b)]
        level_a[:, at(b)] = new
        pack_b[:, at(b)] = (scale_ref[:, at(b)] * new).astype(bf16)

    def products(b, count):
        image = jnp.concatenate([operate(pack_b, b + u) for u in range(count)], axis=1)
        high, low = split(level_a[:, columns(lane(b), count * BAND)])
        left = jnp.concatenate([high, *split(image)], axis=0)
        right = jnp.concatenate([high, low], axis=0)
        return lax.dot_general(left, right, (((1,), (1,)), ((), ())), preferred_element_type=f32)

    return pack0, level1, level2, level3, products


def combine(sums):
    cross = sums[:VECS, VECS:]
    gram = sums[:VECS, :VECS] + cross + cross.T
    image = sums[VECS : 2 * VECS, :] + sums[2 * VECS :, :]
    image = (image[:, :VECS] + image[:, VECS:]).T
    return jnp.concatenate([gram, image], axis=1)


def interior_kernel(
    emb_ref, id_ref, chunk_ref,
    level_hbm, gram_ref,
    lhs_ref, rhs_ref, weight_ref, scale_ref, carry_ref, start_ref, pack_a, pack_b, level_a, level_b, sems,
):
    step = pl.program_id(0)
    count = pl.num_programs(0)
    own = weight_ref.shape[0] - 2
    @pl.when(step == 0)
    def _():
        carry_ref[...] = jnp.zeros_like(carry_ref)
        lhs_ref[:, :BAND] = jnp.zeros((DEPTH, BAND), bf16)
        rhs_ref[:, :BAND] = jnp.zeros((DEPTH, BAND), bf16)

    start_ref[:, columns(step * CHUNK + BAND, CHUNK)] = chunk_ref[...]
    for j in range(CHUNK // 256):
        here = slice(j * 256, j * 256 + 256)
        prepare(emb_ref[:, here], id_ref[:, here] + 1, 1 + 2 * j, lhs_ref, rhs_ref)
    carried = carry_ref[...]
    for i in range(CHUNK_BLOCKS // 2):
        carried = affinity_pair(
            2 * i, step * CHUNK_BLOCKS + 2 * i, carried, True, lhs_ref, rhs_ref, weight_ref, scale_ref
        )
    carry_ref[...] = carried
    lhs_ref[:, :BAND] = lhs_ref[:, CHUNK:]
    rhs_ref[:, :BAND] = rhs_ref[:, CHUNK:]

    @pl.when(step == count - 1)
    def _():
        pack0, level1, level2, level3, products = operators(
            lambda b: b * BAND, weight_ref, scale_ref, start_ref, pack_a, pack_b, level_a, level_b
        )
        for one in (pack0, level1, level2, level3):
            for b in range(2, own):
                one(b)
        inner = slice((HALO_BLOCKS + 1) * BAND, (own + 1 - HALO_BLOCKS) * BAND)
        outer = slice(HALO_BLOCKS * BAND, (own - HALO_BLOCKS) * BAND)
        out_copy = pltpu.make_async_copy(level_a.at[:, inner], level_hbm.at[:, outer], sems)
        out_copy.start()
        sums = jnp.zeros((3 * VECS, 2 * VECS), f32)
        for b in range(HALO_BLOCKS + 1, own + 1 - HALO_BLOCKS, GRAM_BLOCKS):
            sums += products(b, min(GRAM_BLOCKS, own + 1 - HALO_BLOCKS - b))
        gram_ref[...] = combine(sums)
        out_copy.wait()


def interior(emb, ids, start):
    rows = emb.shape[1]
    blocks = rows // BAND + 1
    return pl.pallas_call(
        interior_kernel,
        grid=(rows // CHUNK,),
        in_specs=[
            pl.BlockSpec((EMB, CHUNK), lambda i: (0, i)),
            pl.BlockSpec((1, CHUNK), lambda i: (0, i)),
            pl.BlockSpec((VECS, CHUNK), lambda i: (0, i)),
        ],
        out_specs=[pl.BlockSpec(memory_space=pl.ANY), pl.BlockSpec(memory_space=pltpu.VMEM)],
        out_shape=[
            jax.ShapeDtypeStruct((VECS, rows), f32),
            jax.ShapeDtypeStruct((VECS, 2 * VECS), f32),
        ],
        scratch_shapes=[
            pltpu.VMEM((DEPTH, CHUNK + BAND), bf16),
            pltpu.VMEM((DEPTH, CHUNK + BAND), bf16),
            pltpu.VMEM((blocks + 1, 3 * BAND, BAND), bf16),
            pltpu.VMEM((1, blocks * BAND), f32),
            pltpu.VMEM((1, BAND), f32),
            pltpu.VMEM((VECS, blocks * BAND), bf16),
            pltpu.VMEM((VECS, blocks * BAND), bf16),
            pltpu.VMEM((VECS, blocks * BAND), bf16),
            pltpu.VMEM((VECS, blocks * BAND), f32),
            pltpu.VMEM((VECS, blocks * BAND), f32),
            pltpu.SemaphoreType.DMA,
        ],
        compiler_params=pltpu.CompilerParams(vmem_limit_bytes=VMEM_BYTES, dimension_semantics=("arbitrary",)),
        name="interior",
    )(emb, ids, start)


def edges_kernel(emb_hbm, id_hbm, start_hbm, first_ref, last_ref, label_ref, sems):
    rows = emb_hbm.shape[1]
    copies = []
    for side, (target, begin) in enumerate(((first_ref, 0), (last_ref, rows - HALO))):
        there = slice(begin, begin + HALO)
        copies += [
            pltpu.make_async_copy(id_hbm.at[:, there], label_ref.at[side], sems.at[side, 0]),
            pltpu.make_async_copy(emb_hbm.at[:, there], target.at[:EMB, :], sems.at[side, 1]),
            pltpu.make_async_copy(start_hbm.at[:, there], target.at[EMB : EMB + VECS, :], sems.at[side, 2]),
        ]
    for copy in copies:
        copy.start()
    for side, target in enumerate((first_ref, last_ref)):
        copies[3 * side].wait()
        labels = jnp.broadcast_to(label_ref[side] + 1, (16, HALO)).astype(f32)
        target[EMB + VECS :, :] = labels.astype(bf16)
        copies[3 * side + 1].wait()
        copies[3 * side + 2].wait()


def edges(emb, ids, start):
    whole = pl.BlockSpec(memory_space=pltpu.VMEM)
    away = pl.BlockSpec(memory_space=pl.ANY)
    return pl.pallas_call(
        edges_kernel,
        in_specs=[away, away, away],
        out_specs=[whole, whole],
        out_shape=[jax.ShapeDtypeStruct((EMB + VECS + 16, HALO), bf16)] * 2,
        scratch_shapes=[pltpu.VMEM((2, 1, HALO), jnp.int32), pltpu.SemaphoreType.DMA((2, 3))],
        compiler_params=pltpu.CompilerParams(vmem_limit_bytes=VMEM_BYTES),
        name="edges",
    )(emb, ids, start)


INSIDE = 2 * HALO
ENDS = 2 * (HALO + INSIDE)
END_BLOCKS = ENDS // BAND


def ends_kernel(
    low_ref, high_ref, sums_ref, id_hbm, emb_hbm, start_hbm, level_in,
    level_hbm, gram_ref,
    id_ref, emb_ref, lhs_ref, rhs_ref, weight_ref, scale_ref, start_ref, pack_a, pack_b, level_a, level_b, sems,
):
    rows = emb_hbm.shape[1]
    first = slice(0, INSIDE)
    last = slice(rows - INSIDE, rows)
    first_at = slice(HALO, HALO + INSIDE)
    last_at = slice(HALO + INSIDE, HALO + 2 * INSIDE)
    copies = [
        pltpu.make_async_copy(source.at[:, there], target.at[:, here], sems.at[i])
        for i, (source, there, target, here) in enumerate(
            (
                (id_hbm, first, id_ref, first_at),
                (id_hbm, last, id_ref, last_at),
                (emb_hbm, first, emb_ref, first_at),
                (emb_hbm, last, emb_ref, last_at),
                (start_hbm, first, start_ref, first_at),
                (start_hbm, last, start_ref, last_at),
            )
        )
    ]
    for copy in copies:
        copy.start()
    for ref, begin in ((low_ref, 0), (high_ref, ENDS - HALO)):
        here = slice(begin, begin + HALO)
        emb_ref[:, here] = ref[:EMB, :]
        start_ref[:, here] = ref[EMB : EMB + VECS, :]
        id_ref[:, here] = ref[EMB + VECS :, :].astype(f32)[:1].astype(jnp.int32) - 1
    for copy in copies[:4]:
        copy.wait()
    for j in range(ENDS // 256):
        here = slice(j * 256, j * 256 + 256)
        prepare(emb_ref[:, here], id_ref[:, here] + 1, 2 * j, lhs_ref, rhs_ref)
    carried = jnp.zeros((1, BAND), f32)
    for i in range(END_BLOCKS // 2):
        carried = affinity_pair(
            2 * i, 2 * i, carried, i < END_BLOCKS // 2 - 1, lhs_ref, rhs_ref, weight_ref, scale_ref
        )
    pack0, level1, level2, level3, products = operators(
        lambda b: b * BAND, weight_ref, scale_ref, start_ref, pack_a, pack_b, level_a, level_b
    )
    half = END_BLOCKS // 2
    for copy in copies[4:]:
        copy.wait()
    for margin, one in ((1, pack0), (2, level1), (3, level2), (4, level3)):
        for b in (*range(margin, half - margin), *range(half + margin, END_BLOCKS - margin)):
            one(b)
    outs = [
        pltpu.make_async_copy(level_a.at[:, here], level_hbm.at[:, there], sems.at[i])
        for i, (here, there) in enumerate(
            (
                (slice(HALO, 2 * HALO), slice(0, HALO)),
                (slice(ENDS - 2 * HALO, ENDS - HALO), slice(rows - HALO, rows)),
            )
        )
    ]
    for copy in outs:
        copy.start()
    sums = products(HALO_BLOCKS, HALO_BLOCKS) + products(END_BLOCKS - 2 * HALO_BLOCKS, HALO_BLOCKS)
    gram_ref[...] = sums_ref[...] + combine(sums)
    for copy in outs:
        copy.wait()


def ends(low, high, ids, sums, emb, start, level):
    whole = pl.BlockSpec(memory_space=pltpu.VMEM)
    away = pl.BlockSpec(memory_space=pl.ANY)
    return pl.pallas_call(
        ends_kernel,
        in_specs=[whole, whole, whole, away, away, away, away],
        out_specs=[away, whole],
        out_shape=[
            jax.ShapeDtypeStruct(level.shape, f32),
            jax.ShapeDtypeStruct((VECS, 2 * VECS), f32),
        ],
        input_output_aliases={6: 0},
        scratch_shapes=[
            pltpu.VMEM((1, ENDS), jnp.int32),
            pltpu.VMEM((EMB, ENDS), bf16),
            pltpu.VMEM((DEPTH, ENDS), bf16),
            pltpu.VMEM((DEPTH, ENDS), bf16),
            pltpu.VMEM((END_BLOCKS, 3 * BAND, BAND), bf16),
            pltpu.VMEM((1, ENDS), f32),
            pltpu.VMEM((VECS, ENDS), bf16),
            pltpu.VMEM((VECS, ENDS), bf16),
            pltpu.VMEM((VECS, ENDS), bf16),
            pltpu.VMEM((VECS, ENDS), f32),
            pltpu.VMEM((VECS, ENDS), f32),
            pltpu.SemaphoreType.DMA((6,)),
        ],
        compiler_params=pltpu.CompilerParams(vmem_limit_bytes=VMEM_BYTES),
        name="ends",
    )(low, high, sums, ids, emb, start, level)


def total(x, axes):
    for axis in axes:
        size = lax.axis_size(axis)
        if size & (size - 1):
            x = lax.psum(x, axis)
            continue
        stride = 1
        while stride < size:
            x = x + lax.ppermute(x, axis, [(i, i ^ stride) for i in range(size)])
            stride *= 2
    return x


def basis_kernel(gram_ref, level_hbm, basis_ref, ritz_ref, inverse_ref, level_ref, sem):
    width = basis_ref.shape[1]

    @pl.when(pl.program_id(0) == 0)
    def _():
        copy = pltpu.make_async_copy(level_hbm, level_ref, sem)
        copy.start()
        row = lax.broadcasted_iota(jnp.int32, (VECS, 2 * VECS), 0)
        col = lax.broadcasted_iota(jnp.int32, (VECS, 2 * VECS), 1)
        work = jnp.where(col < VECS, gram_ref[...], jnp.where(col == row + VECS, 1.0, 0.0))
        for k in range(0, VECS, GROUP):
            spread = [jnp.broadcast_to(work[:, j : j + 1], work.shape) for j in range(k, k + GROUP)]
            pivots = [work[j : j + 1, :] for j in range(k, k + GROUP)]
            for j in range(GROUP):
                factor = jnp.where(row > k + j, spread[j] * (1.0 / spread[j][k + j : k + j + 1, :]), 0.0)
                for m in range(j + 1, GROUP):
                    spread[m] = spread[m] - factor * spread[m][k + j : k + j + 1, :]
                    pivots[m] = pivots[m] - factor[k + m : k + m + 1, :] * pivots[j]
                work = work - factor * pivots[j]
        diagonal = jnp.sum(jnp.where(row == col, work, 0.0), axis=1, keepdims=True)
        inverse = (work * lax.rsqrt(diagonal))[:, VECS:]
        image = gram_ref[:, VECS:]
        exact = lax.Precision.HIGHEST
        left = jnp.dot(inverse, image, precision=exact, preferred_element_type=f32)
        ritz_ref[...] = lax.dot_general(
            left, inverse, (((1,), (1,)), ((), ())), precision=exact, preferred_element_type=f32
        )
        high, low = split(inverse)
        inverse_ref[...] = jnp.concatenate([high, high, low], axis=1)
        copy.wait()

    high, low = split(level_ref[:, columns(pl.program_id(0) * width, width)])
    basis_ref[...] = jnp.dot(
        inverse_ref[...], jnp.concatenate([high, low, high], axis=0), preferred_element_type=f32
    )


def orthonormal(sums, level):
    rows = level.shape[1]
    width = 2 * CHUNK
    whole = pl.BlockSpec(memory_space=pltpu.VMEM)
    return pl.pallas_call(
        basis_kernel,
        grid=(rows // width,),
        in_specs=[whole, pl.BlockSpec(memory_space=pl.ANY)],
        out_specs=[pl.BlockSpec((VECS, width), lambda i: (0, i)), whole],
        out_shape=[
            jax.ShapeDtypeStruct((VECS, rows), f32),
            jax.ShapeDtypeStruct((VECS, VECS), f32),
        ],
        scratch_shapes=[
            pltpu.VMEM((VECS, 3 * VECS), bf16),
            pltpu.VMEM((VECS, rows), f32),
            pltpu.SemaphoreType.DMA,
        ],
        compiler_params=pltpu.CompilerParams(vmem_limit_bytes=VMEM_BYTES),
        name="basis",
    )(sums, level)


def per_device(embeddings, stream_ids, start_block):
    emb, start = embeddings.T, start_block.T
    rows = emb.shape[1]
    ids = stream_ids.reshape(1, rows)

    first, last = edges(emb, ids, start)
    axes = ("ta", "au")
    steps = range(lax.axis_size(axes) - 1)
    low = lax.ppermute(last, axes, [(i, i + 1) for i in steps])
    high = lax.ppermute(first, axes, [(i + 1, i) for i in steps])
    level, sums = interior(emb, ids, start)
    level, sums = ends(low, high, ids, sums, emb, start, level)
    basis, ritz = orthonormal(total(sums, axes), level)
    return basis.T, ritz


def solution(mesh):
    placed = (P(("ta", "au"), None), P(("ta", "au")), P(("ta", "au"), None))
    return jax.shard_map(
        per_device,
        mesh=mesh,
        in_specs=placed,
        out_specs=(P(("ta", "au"), None), P()),
        check_vma=False,
    )
```

```python
import jax
import jax.numpy as jnp
from jax import lax
from jax.experimental import pallas as pl
from jax.experimental.pallas import tpu as pltpu
from jax.sharding import PartitionSpec as P

BAND = 128
HALO_BLOCKS = 5
HALO = HALO_BLOCKS * BAND
EMB = 192
VECS = 64
CHUNK_BLOCKS = 32
CHUNK = CHUNK_BLOCKS * BAND
DEPTH = 256
PENALTY = 64.0
GROUP = 8
GRAM_BLOCKS = 26
EXPONENT = 4.328085122666891
VMEM_BYTES = 62 << 20

bf16 = jnp.bfloat16
f32 = jnp.float32


def columns(start, size):
    if isinstance(start, int):
        return slice(start, start + size)
    return pl.ds(pl.multiple_of(start, BAND), size)


def split(x):
    high = x.astype(bf16)
    return high, (x - high.astype(f32)).astype(bf16)


def prepare(values, labels, slot, lhs_ref, rhs_ref):
    width = values.shape[1]
    values = values.astype(f32)
    normed = (values * lax.rsqrt(jnp.sum(values * values, axis=0, keepdims=True) + 1e-06)).astype(bf16)
    shift = lax.broadcasted_iota(jnp.int32, (16, width), 0)
    bits = (lax.shift_right_logical(jnp.broadcast_to(labels, (16, width)), shift) & 1).astype(f32)
    unset = 1.0 - bits
    first = jnp.where(shift == 0, 1.0, 0.0)
    zeros = jnp.zeros((16, width), bf16)
    rhs = jnp.concatenate(
        [normed, (-PENALTY * unset).astype(bf16), (-PENALTY * bits).astype(bf16), (-first).astype(bf16), zeros], axis=0
    )
    lhs = jnp.concatenate([normed, bits.astype(bf16), unset.astype(bf16), first.astype(bf16), zeros], axis=0)
    rhs_ref[:, slot * BAND : slot * BAND + width] = rhs
    lhs_ref[:, slot * BAND : slot * BAND + width] = lhs


def affinity_pair(slot, block, carried, right, lhs_ref, rhs_ref, weight_ref, scale_ref):
    row = lax.broadcasted_iota(jnp.int32, (BAND, BAND), 0)
    col = lax.broadcasted_iota(jnp.int32, (BAND, BAND), 1)
    for i in range(2):
        here = slice((slot + i) * BAND, (slot + i + 1) * BAND)
        both = right or i == 0
        there = slice((slot + i) * BAND, (slot + i + 1 + both) * BAND)
        z = lax.dot_general(lhs_ref[:, there], rhs_ref[:, here], (((0,), (0,)), ((), ())), preferred_element_type=f32)
        e = jnp.exp2(z * EXPONENT)
        own = e[:BAND].astype(bf16)
        weight_ref[block + i, BAND : 2 * BAND, :] = own
        if not both:
            return carried
        after = jnp.where(row <= col, e[BAND:], 0.0).astype(bf16)
        before = after.T
        weight_ref[block + i, 2 * BAND :, :] = after
        weight_ref[block + i + 1, :BAND, :] = before
        degree = jnp.sum(own.astype(f32) + after.astype(f32), axis=0, keepdims=True) + carried
        scale_ref[:, columns((block + i) * BAND, BAND)] = lax.rsqrt(degree)
        carried = jnp.sum(before.astype(f32), axis=0, keepdims=True)
    return carried


def operators(lane, weight_ref, scale_ref, start_ref, pack_a, pack_b, level_a, level_b):
    def at(b):
        return columns(lane(b), BAND)

    def pack0(b):
        pack_a[:, at(b)] = (scale_ref[:, at(b)] * start_ref[:, at(b)].astype(f32)).astype(bf16)

    def operate(packed, b):
        window = packed[:, columns(lane(b - 1), 3 * BAND)]
        return scale_ref[:, at(b)] * jnp.dot(window, weight_ref[b], preferred_element_type=f32)

    def level1(b):
        new = operate(pack_a, b) * (1.0 / 0.6) - 0.5 * start_ref[:, at(b)].astype(f32)
        level_a[:, at(b)] = new
        pack_b[:, at(b)] = (scale_ref[:, at(b)] * new).astype(bf16)

    def level2(b):
        new = operate(pack_b, b) * (2.0 / 0.6) - level_a[:, at(b)] - start_ref[:, at(b)].astype(f32)
        level_b[:, at(b)] = new
        pack_a[:, at(b)] = (scale_ref[:, at(b)] * new).astype(bf16)

    def level3(b):
        new = operate(pack_a, b) * (2.0 / 0.6) - level_b[:, at(b)] - level_a[:, at(b)]
        level_a[:, at(b)] = new
        pack_b[:, at(b)] = (scale_ref[:, at(b)] * new).astype(bf16)

    def products(b, count):
        image = jnp.concatenate([operate(pack_b, b + u) for u in range(count)], axis=1)
        high, low = split(level_a[:, columns(lane(b), count * BAND)])
        left = jnp.concatenate([high, *split(image)], axis=0)
        right = jnp.concatenate([high, low], axis=0)
        return lax.dot_general(left, right, (((1,), (1,)), ((), ())), preferred_element_type=f32)

    return pack0, level1, level2, level3, products


def combine(sums):
    cross = sums[:VECS, VECS:]
    gram = sums[:VECS, :VECS] + cross + cross.T
    image = sums[VECS : 2 * VECS, :] + sums[2 * VECS :, :]
    image = (image[:, :VECS] + image[:, VECS:]).T
    return jnp.concatenate([gram, image], axis=1)


def interior_kernel(
    emb_ref, id_ref, chunk_ref,
    level_hbm, gram_ref,
    lhs_ref, rhs_ref, weight_ref, scale_ref, carry_ref, start_ref, pack_a, pack_b, level_a, level_b, sems,
):
    step = pl.program_id(0)
    count = pl.num_programs(0)
    own = weight_ref.shape[0] - 2
    @pl.when(step == 0)
    def _():
        carry_ref[...] = jnp.zeros_like(carry_ref)
        lhs_ref[:, :BAND] = jnp.zeros((DEPTH, BAND), bf16)
        rhs_ref[:, :BAND] = jnp.zeros((DEPTH, BAND), bf16)

    start_ref[:, columns(step * CHUNK + BAND, CHUNK)] = chunk_ref[...]
    for j in range(CHUNK // 256):
        here = slice(j * 256, j * 256 + 256)
        prepare(emb_ref[:, here], id_ref[:, here] + 1, 1 + 2 * j, lhs_ref, rhs_ref)
    carried = carry_ref[...]
    for i in range(CHUNK_BLOCKS // 2):
        carried = affinity_pair(
            2 * i, step * CHUNK_BLOCKS + 2 * i, carried, True, lhs_ref, rhs_ref, weight_ref, scale_ref
        )
    carry_ref[...] = carried
    lhs_ref[:, :BAND] = lhs_ref[:, CHUNK:]
    rhs_ref[:, :BAND] = rhs_ref[:, CHUNK:]

    @pl.when(step == count - 1)
    def _():
        pack0, level1, level2, level3, products = operators(
            lambda b: b * BAND, weight_ref, scale_ref, start_ref, pack_a, pack_b, level_a, level_b
        )
        for one in (pack0, level1, level2, level3):
            for b in range(2, own):
                one(b)
        inner = slice((HALO_BLOCKS + 1) * BAND, (own + 1 - HALO_BLOCKS) * BAND)
        outer = slice(HALO_BLOCKS * BAND, (own - HALO_BLOCKS) * BAND)
        out_copy = pltpu.make_async_copy(level_a.at[:, inner], level_hbm.at[:, outer], sems)
        out_copy.start()
        sums = jnp.zeros((3 * VECS, 2 * VECS), f32)
        for b in range(HALO_BLOCKS + 1, own + 1 - HALO_BLOCKS, GRAM_BLOCKS):
            sums += products(b, min(GRAM_BLOCKS, own + 1 - HALO_BLOCKS - b))
        gram_ref[...] = combine(sums)
        out_copy.wait()


def interior(emb, ids, start):
    rows = emb.shape[1]
    blocks = rows // BAND + 1
    return pl.pallas_call(
        interior_kernel,
        grid=(rows // CHUNK,),
        in_specs=[
            pl.BlockSpec((EMB, CHUNK), lambda i: (0, i)),
            pl.BlockSpec((1, CHUNK), lambda i: (0, i)),
            pl.BlockSpec((VECS, CHUNK), lambda i: (0, i)),
        ],
        out_specs=[pl.BlockSpec(memory_space=pl.ANY), pl.BlockSpec(memory_space=pltpu.VMEM)],
        out_shape=[
            jax.ShapeDtypeStruct((VECS, rows), f32),
            jax.ShapeDtypeStruct((VECS, 2 * VECS), f32),
        ],
        scratch_shapes=[
            pltpu.VMEM((DEPTH, CHUNK + BAND), bf16),
            pltpu.VMEM((DEPTH, CHUNK + BAND), bf16),
            pltpu.VMEM((blocks + 1, 3 * BAND, BAND), bf16),
            pltpu.VMEM((1, blocks * BAND), f32),
            pltpu.VMEM((1, BAND), f32),
            pltpu.VMEM((VECS, blocks * BAND), bf16),
            pltpu.VMEM((VECS, blocks * BAND), bf16),
            pltpu.VMEM((VECS, blocks * BAND), bf16),
            pltpu.VMEM((VECS, blocks * BAND), f32),
            pltpu.VMEM((VECS, blocks * BAND), f32),
            pltpu.SemaphoreType.DMA,
        ],
        compiler_params=pltpu.CompilerParams(vmem_limit_bytes=VMEM_BYTES, dimension_semantics=("arbitrary",)),
        name="interior",
    )(emb, ids, start)


def edges_kernel(emb_hbm, id_hbm, start_hbm, first_ref, last_ref, label_ref, sems):
    rows = emb_hbm.shape[1]
    copies = []
    for side, (target, begin) in enumerate(((first_ref, 0), (last_ref, rows - HALO))):
        there = slice(begin, begin + HALO)
        copies += [
            pltpu.make_async_copy(id_hbm.at[:, there], label_ref.at[side], sems.at[side, 0]),
            pltpu.make_async_copy(emb_hbm.at[:, there], target.at[:EMB, :], sems.at[side, 1]),
            pltpu.make_async_copy(start_hbm.at[:, there], target.at[EMB : EMB + VECS, :], sems.at[side, 2]),
        ]
    for copy in copies:
        copy.start()
    for side, target in enumerate((first_ref, last_ref)):
        copies[3 * side].wait()
        labels = jnp.broadcast_to(label_ref[side] + 1, (16, HALO)).astype(f32)
        target[EMB + VECS :, :] = labels.astype(bf16)
        copies[3 * side + 1].wait()
        copies[3 * side + 2].wait()


def edges(emb, ids, start):
    whole = pl.BlockSpec(memory_space=pltpu.VMEM)
    away = pl.BlockSpec(memory_space=pl.ANY)
    return pl.pallas_call(
        edges_kernel,
        in_specs=[away, away, away],
        out_specs=[whole, whole],
        out_shape=[jax.ShapeDtypeStruct((EMB + VECS + 16, HALO), bf16)] * 2,
        scratch_shapes=[pltpu.VMEM((2, 1, HALO), jnp.int32), pltpu.SemaphoreType.DMA((2, 3))],
        compiler_params=pltpu.CompilerParams(vmem_limit_bytes=VMEM_BYTES),
        name="edges",
    )(emb, ids, start)


INSIDE = 2 * HALO
ENDS = 2 * (HALO + INSIDE)
END_BLOCKS = ENDS // BAND


def ends_kernel(
    low_ref, high_ref, sums_ref, id_hbm, emb_hbm, start_hbm, level_in,
    level_hbm, gram_ref,
    id_ref, emb_ref, lhs_ref, rhs_ref, weight_ref, scale_ref, start_ref, pack_a, pack_b, level_a, level_b, sems,
):
    rows = emb_hbm.shape[1]
    first = slice(0, INSIDE)
    last = slice(rows - INSIDE, rows)
    first_at = slice(HALO, HALO + INSIDE)
    last_at = slice(HALO + INSIDE, HALO + 2 * INSIDE)
    copies = [
        pltpu.make_async_copy(source.at[:, there], target.at[:, here], sems.at[i])
        for i, (source, there, target, here) in enumerate(
            (
                (id_hbm, first, id_ref, first_at),
                (id_hbm, last, id_ref, last_at),
                (emb_hbm, first, emb_ref, first_at),
                (emb_hbm, last, emb_ref, last_at),
                (start_hbm, first, start_ref, first_at),
                (start_hbm, last, start_ref, last_at),
            )
        )
    ]
    for copy in copies:
        copy.start()
    for ref, begin in ((low_ref, 0), (high_ref, ENDS - HALO)):
        here = slice(begin, begin + HALO)
        emb_ref[:, here] = ref[:EMB, :]
        start_ref[:, here] = ref[EMB : EMB + VECS, :]
        id_ref[:, here] = ref[EMB + VECS :, :].astype(f32)[:1].astype(jnp.int32) - 1
    for copy in copies[:4]:
        copy.wait()
    for j in range(ENDS // 256):
        here = slice(j * 256, j * 256 + 256)
        prepare(emb_ref[:, here], id_ref[:, here] + 1, 2 * j, lhs_ref, rhs_ref)
    carried = jnp.zeros((1, BAND), f32)
    for i in range(END_BLOCKS // 2):
        carried = affinity_pair(
            2 * i, 2 * i, carried, i < END_BLOCKS // 2 - 1, lhs_ref, rhs_ref, weight_ref, scale_ref
        )
    pack0, level1, level2, level3, products = operators(
        lambda b: b * BAND, weight_ref, scale_ref, start_ref, pack_a, pack_b, level_a, level_b
    )
    half = END_BLOCKS // 2
    for copy in copies[4:]:
        copy.wait()
    for margin, one in ((1, pack0), (2, level1), (3, level2), (4, level3)):
        for b in (*range(margin, half - margin), *range(half + margin, END_BLOCKS - margin)):
            one(b)
    outs = [
        pltpu.make_async_copy(level_a.at[:, here], level_hbm.at[:, there], sems.at[i])
        for i, (here, there) in enumerate(
            (
                (slice(HALO, 2 * HALO), slice(0, HALO)),
                (slice(ENDS - 2 * HALO, ENDS - HALO), slice(rows - HALO, rows)),
            )
        )
    ]
    for copy in outs:
        copy.start()
    sums = products(HALO_BLOCKS, HALO_BLOCKS) + products(END_BLOCKS - 2 * HALO_BLOCKS, HALO_BLOCKS)
    gram_ref[...] = sums_ref[...] + combine(sums)
    for copy in outs:
        copy.wait()


def ends(low, high, ids, sums, emb, start, level):
    whole = pl.BlockSpec(memory_space=pltpu.VMEM)
    away = pl.BlockSpec(memory_space=pl.ANY)
    return pl.pallas_call(
        ends_kernel,
        in_specs=[whole, whole, whole, away, away, away, away],
        out_specs=[away, whole],
        out_shape=[
            jax.ShapeDtypeStruct(level.shape, f32),
            jax.ShapeDtypeStruct((VECS, 2 * VECS), f32),
        ],
        input_output_aliases={6: 0},
        scratch_shapes=[
            pltpu.VMEM((1, ENDS), jnp.int32),
            pltpu.VMEM((EMB, ENDS), bf16),
            pltpu.VMEM((DEPTH, ENDS), bf16),
            pltpu.VMEM((DEPTH, ENDS), bf16),
            pltpu.VMEM((END_BLOCKS, 3 * BAND, BAND), bf16),
            pltpu.VMEM((1, ENDS), f32),
            pltpu.VMEM((VECS, ENDS), bf16),
            pltpu.VMEM((VECS, ENDS), bf16),
            pltpu.VMEM((VECS, ENDS), bf16),
            pltpu.VMEM((VECS, ENDS), f32),
            pltpu.VMEM((VECS, ENDS), f32),
            pltpu.SemaphoreType.DMA((6,)),
        ],
        compiler_params=pltpu.CompilerParams(vmem_limit_bytes=VMEM_BYTES),
        name="ends",
    )(low, high, sums, ids, emb, start, level)


def total(x, axes):
    for axis in axes:
        size = lax.axis_size(axis)
        if size & (size - 1):
            x = lax.psum(x, axis)
            continue
        stride = 1
        while stride < size:
            x = x + lax.ppermute(x, axis, [(i, i ^ stride) for i in range(size)])
            stride *= 2
    return x


def basis_kernel(gram_ref, level_hbm, basis_ref, ritz_ref, inverse_ref, level_ref, sems):
    step = pl.program_id(0)
    width = basis_ref.shape[1]

    def fetch(i):
        here = columns(i * width, width)
        return pltpu.make_async_copy(level_hbm.at[:, here], level_ref.at[:, here], sems.at[i])

    @pl.when(step == 0)
    def _():
        for i in range(level_ref.shape[1] // width):
            fetch(i).start()
        row = lax.broadcasted_iota(jnp.int32, (VECS, 2 * VECS), 0)
        col = lax.broadcasted_iota(jnp.int32, (VECS, 2 * VECS), 1)
        work = jnp.where(col < VECS, gram_ref[...], jnp.where(col == row + VECS, 1.0, 0.0))
        for k in range(0, VECS, GROUP):
            spread = [jnp.broadcast_to(work[:, j : j + 1], work.shape) for j in range(k, k + GROUP)]
            pivots = [work[j : j + 1, :] for j in range(k, k + GROUP)]
            for j in range(GROUP):
                factor = jnp.where(row > k + j, spread[j] * (1.0 / spread[j][k + j : k + j + 1, :]), 0.0)
                for m in range(j + 1, GROUP):
                    spread[m] = spread[m] - factor * spread[m][k + j : k + j + 1, :]
                    pivots[m] = pivots[m] - factor[k + m : k + m + 1, :] * pivots[j]
                work = work - factor * pivots[j]
        diagonal = jnp.sum(jnp.where(row == col, work, 0.0), axis=1, keepdims=True)
        inverse = (work * lax.rsqrt(diagonal))[:, VECS:]
        image = gram_ref[:, VECS:]
        exact = lax.Precision.HIGHEST
        left = jnp.dot(inverse, image, precision=exact, preferred_element_type=f32)
        ritz_ref[...] = lax.dot_general(
            left, inverse, (((1,), (1,)), ((), ())), precision=exact, preferred_element_type=f32
        )
        high, low = split(inverse)
        inverse_ref[...] = jnp.concatenate([high, high, low], axis=1)

    fetch(step).wait()
    high, low = split(level_ref[:, columns(step * width, width)])
    basis_ref[...] = jnp.dot(
        inverse_ref[...], jnp.concatenate([high, low, high], axis=0), preferred_element_type=f32
    )


def orthonormal(sums, level):
    rows = level.shape[1]
    width = 2 * CHUNK
    whole = pl.BlockSpec(memory_space=pltpu.VMEM)
    return pl.pallas_call(
        basis_kernel,
        grid=(rows // width,),
        in_specs=[whole, pl.BlockSpec(memory_space=pl.ANY)],
        out_specs=[pl.BlockSpec((VECS, width), lambda i: (0, i)), whole],
        out_shape=[
            jax.ShapeDtypeStruct((VECS, rows), f32),
            jax.ShapeDtypeStruct((VECS, VECS), f32),
        ],
        scratch_shapes=[
            pltpu.VMEM((VECS, 3 * VECS), bf16),
            pltpu.VMEM((VECS, rows), f32),
            pltpu.SemaphoreType.DMA((rows // width,)),
        ],
        compiler_params=pltpu.CompilerParams(vmem_limit_bytes=VMEM_BYTES),
        name="basis",
    )(sums, level)


def per_device(embeddings, stream_ids, start_block):
    emb, start = embeddings.T, start_block.T
    rows = emb.shape[1]
    ids = stream_ids.reshape(1, rows)

    first, last = edges(emb, ids, start)
    axes = ("ta", "au")
    steps = range(lax.axis_size(axes) - 1)
    low = lax.ppermute(last, axes, [(i, i + 1) for i in steps])
    high = lax.ppermute(first, axes, [(i + 1, i) for i in steps])
    level, sums = interior(emb, ids, start)
    level, sums = ends(low, high, ids, sums, emb, start, level)
    basis, ritz = orthonormal(total(sums, axes), level)
    return basis.T, ritz


def solution(mesh):
    placed = (P(("ta", "au"), None), P(("ta", "au")), P(("ta", "au"), None))
    return jax.shard_map(
        per_device,
        mesh=mesh,
        in_specs=placed,
        out_specs=(P(("ta", "au"), None), P()),
        check_vma=False,
    )
```

```python
import jax
import jax.numpy as jnp
from jax import lax
from jax.experimental import pallas as pl
from jax.experimental.pallas import tpu as pltpu
from jax.sharding import PartitionSpec as P

BAND = 128
HALO_BLOCKS = 5
HALO = HALO_BLOCKS * BAND
EMB = 192
VECS = 64
CHUNK_BLOCKS = 32
CHUNK = CHUNK_BLOCKS * BAND
DEPTH = 256
PENALTY = 64.0
GROUP = 8
GRAM_BLOCKS = 26
EXPONENT = 4.328085122666891
VMEM_BYTES = 62 << 20

bf16 = jnp.bfloat16
f32 = jnp.float32


def columns(start, size):
    if isinstance(start, int):
        return slice(start, start + size)
    return pl.ds(pl.multiple_of(start, BAND), size)


def split(x):
    high = x.astype(bf16)
    return high, (x - high.astype(f32)).astype(bf16)


def prepare(values, labels, slot, lhs_ref, rhs_ref):
    width = values.shape[1]
    values = values.astype(f32)
    normed = (values * lax.rsqrt(jnp.sum(values * values, axis=0, keepdims=True) + 1e-06)).astype(bf16)
    shift = lax.broadcasted_iota(jnp.int32, (16, width), 0)
    bits = (lax.shift_right_logical(jnp.broadcast_to(labels, (16, width)), shift) & 1).astype(f32)
    unset = 1.0 - bits
    first = jnp.where(shift == 0, 1.0, 0.0)
    zeros = jnp.zeros((16, width), bf16)
    rhs = jnp.concatenate(
        [normed, (-PENALTY * unset).astype(bf16), (-PENALTY * bits).astype(bf16), (-first).astype(bf16), zeros], axis=0
    )
    lhs = jnp.concatenate([normed, bits.astype(bf16), unset.astype(bf16), first.astype(bf16), zeros], axis=0)
    rhs_ref[:, slot * BAND : slot * BAND + width] = rhs
    lhs_ref[:, slot * BAND : slot * BAND + width] = lhs


def affinity_pair(slot, block, carried, right, lhs_ref, rhs_ref, weight_ref, scale_ref):
    row = lax.broadcasted_iota(jnp.int32, (BAND, BAND), 0)
    col = lax.broadcasted_iota(jnp.int32, (BAND, BAND), 1)
    for i in range(2):
        here = slice((slot + i) * BAND, (slot + i + 1) * BAND)
        both = right or i == 0
        there = slice((slot + i) * BAND, (slot + i + 1 + both) * BAND)
        z = lax.dot_general(lhs_ref[:, there], rhs_ref[:, here], (((0,), (0,)), ((), ())), preferred_element_type=f32)
        e = jnp.exp2(z * EXPONENT)
        own = e[:BAND].astype(bf16)
        weight_ref[block + i, BAND : 2 * BAND, :] = own
        if not both:
            return carried
        after = jnp.where(row <= col, e[BAND:], 0.0).astype(bf16)
        before = after.T
        weight_ref[block + i, 2 * BAND :, :] = after
        weight_ref[block + i + 1, :BAND, :] = before
        degree = jnp.sum(own.astype(f32) + after.astype(f32), axis=0, keepdims=True) + carried
        scale_ref[:, columns((block + i) * BAND, BAND)] = lax.rsqrt(degree)
        carried = jnp.sum(before.astype(f32), axis=0, keepdims=True)
    return carried


def operators(lane, weight_ref, scale_ref, start_ref, pack_a, pack_b, level_a, level_b):
    def at(b):
        return columns(lane(b), BAND)

    def pack0(b):
        pack_a[:, at(b)] = (scale_ref[:, at(b)] * start_ref[:, at(b)].astype(f32)).astype(bf16)

    def operate(packed, b):
        window = packed[:, columns(lane(b - 1), 3 * BAND)]
        return scale_ref[:, at(b)] * jnp.dot(window, weight_ref[b], preferred_element_type=f32)

    def level1(b):
        new = operate(pack_a, b) * (1.0 / 0.6) - 0.5 * start_ref[:, at(b)].astype(f32)
        level_a[:, at(b)] = new
        pack_b[:, at(b)] = (scale_ref[:, at(b)] * new).astype(bf16)

    def level2(b):
        new = operate(pack_b, b) * (2.0 / 0.6) - level_a[:, at(b)] - start_ref[:, at(b)].astype(f32)
        level_b[:, at(b)] = new
        pack_a[:, at(b)] = (scale_ref[:, at(b)] * new).astype(bf16)

    def level3(b):
        new = operate(pack_a, b) * (2.0 / 0.6) - level_b[:, at(b)] - level_a[:, at(b)]
        level_a[:, at(b)] = new
        pack_b[:, at(b)] = (scale_ref[:, at(b)] * new).astype(bf16)

    def products(b, count):
        image = jnp.concatenate([operate(pack_b, b + u) for u in range(count)], axis=1)
        high, low = split(level_a[:, columns(lane(b), count * BAND)])
        left = jnp.concatenate([high, *split(image)], axis=0)
        right = jnp.concatenate([high, low], axis=0)
        return lax.dot_general(left, right, (((1,), (1,)), ((), ())), preferred_element_type=f32)

    return pack0, level1, level2, level3, products


def combine(sums):
    cross = sums[:VECS, VECS:]
    gram = sums[:VECS, :VECS] + cross + cross.T
    image = sums[VECS : 2 * VECS, :] + sums[2 * VECS :, :]
    image = (image[:, :VECS] + image[:, VECS:]).T
    return jnp.concatenate([gram, image], axis=1)


def interior_kernel(
    emb_ref, id_ref, chunk_ref,
    level_hbm, gram_ref,
    lhs_ref, rhs_ref, weight_ref, scale_ref, carry_ref, start_ref, pack_a, pack_b, level_a, level_b, sems,
):
    step = pl.program_id(0)
    count = pl.num_programs(0)
    own = weight_ref.shape[0] - 2
    @pl.when(step == 0)
    def _():
        carry_ref[...] = jnp.zeros_like(carry_ref)
        lhs_ref[:, :BAND] = jnp.zeros((DEPTH, BAND), bf16)
        rhs_ref[:, :BAND] = jnp.zeros((DEPTH, BAND), bf16)

    start_ref[:, columns(step * CHUNK + BAND, CHUNK)] = chunk_ref[...]
    for j in range(CHUNK // 256):
        here = slice(j * 256, j * 256 + 256)
        prepare(emb_ref[:, here], id_ref[:, here] + 1, 1 + 2 * j, lhs_ref, rhs_ref)
    carried = carry_ref[...]
    for i in range(CHUNK_BLOCKS // 2):
        carried = affinity_pair(
            2 * i, step * CHUNK_BLOCKS + 2 * i, carried, True, lhs_ref, rhs_ref, weight_ref, scale_ref
        )
    carry_ref[...] = carried
    lhs_ref[:, :BAND] = lhs_ref[:, CHUNK:]
    rhs_ref[:, :BAND] = rhs_ref[:, CHUNK:]

    @pl.when(step == count - 1)
    def _():
        pack0, level1, level2, level3, products = operators(
            lambda b: b * BAND, weight_ref, scale_ref, start_ref, pack_a, pack_b, level_a, level_b
        )
        for one in (pack0, level1, level2, level3):
            for b in range(2, own):
                one(b)
        inner = slice((HALO_BLOCKS + 1) * BAND, (own + 1 - HALO_BLOCKS) * BAND)
        outer = slice(HALO_BLOCKS * BAND, (own - HALO_BLOCKS) * BAND)
        out_copy = pltpu.make_async_copy(level_a.at[:, inner], level_hbm.at[:, outer], sems)
        out_copy.start()
        sums = jnp.zeros((3 * VECS, 2 * VECS), f32)
        for b in range(HALO_BLOCKS + 1, own + 1 - HALO_BLOCKS, GRAM_BLOCKS):
            sums += products(b, min(GRAM_BLOCKS, own + 1 - HALO_BLOCKS - b))
        gram_ref[...] = combine(sums)
        out_copy.wait()


def interior(emb, ids, start):
    rows = emb.shape[1]
    blocks = rows // BAND + 1
    return pl.pallas_call(
        interior_kernel,
        grid=(rows // CHUNK,),
        in_specs=[
            pl.BlockSpec((EMB, CHUNK), lambda i: (0, i)),
            pl.BlockSpec((1, CHUNK), lambda i: (0, i)),
            pl.BlockSpec((VECS, CHUNK), lambda i: (0, i)),
        ],
        out_specs=[pl.BlockSpec(memory_space=pl.ANY), pl.BlockSpec(memory_space=pltpu.VMEM)],
        out_shape=[
            jax.ShapeDtypeStruct((VECS, rows), f32),
            jax.ShapeDtypeStruct((VECS, 2 * VECS), f32),
        ],
        scratch_shapes=[
            pltpu.VMEM((DEPTH, CHUNK + BAND), bf16),
            pltpu.VMEM((DEPTH, CHUNK + BAND), bf16),
            pltpu.VMEM((blocks + 1, 3 * BAND, BAND), bf16),
            pltpu.VMEM((1, blocks * BAND), f32),
            pltpu.VMEM((1, BAND), f32),
            pltpu.VMEM((VECS, blocks * BAND), bf16),
            pltpu.VMEM((VECS, blocks * BAND), bf16),
            pltpu.VMEM((VECS, blocks * BAND), bf16),
            pltpu.VMEM((VECS, blocks * BAND), f32),
            pltpu.VMEM((VECS, blocks * BAND), f32),
            pltpu.SemaphoreType.DMA,
        ],
        compiler_params=pltpu.CompilerParams(vmem_limit_bytes=VMEM_BYTES, dimension_semantics=("arbitrary",)),
        name="interior",
    )(emb, ids, start)


def edges_kernel(emb_hbm, id_hbm, start_hbm, first_ref, last_ref, label_ref, sems):
    rows = emb_hbm.shape[1]
    copies = []
    for side, (target, begin) in enumerate(((first_ref, 0), (last_ref, rows - HALO))):
        there = slice(begin, begin + HALO)
        copies += [
            pltpu.make_async_copy(id_hbm.at[:, there], label_ref.at[side], sems.at[side, 0]),
            pltpu.make_async_copy(emb_hbm.at[:, there], target.at[:EMB, :], sems.at[side, 1]),
            pltpu.make_async_copy(start_hbm.at[:, there], target.at[EMB : EMB + VECS, :], sems.at[side, 2]),
        ]
    for copy in copies:
        copy.start()
    for side, target in enumerate((first_ref, last_ref)):
        copies[3 * side].wait()
        labels = jnp.broadcast_to(label_ref[side] + 1, (16, HALO)).astype(f32)
        target[EMB + VECS :, :] = labels.astype(bf16)
        copies[3 * side + 1].wait()
        copies[3 * side + 2].wait()


def edges(emb, ids, start):
    whole = pl.BlockSpec(memory_space=pltpu.VMEM)
    away = pl.BlockSpec(memory_space=pl.ANY)
    return pl.pallas_call(
        edges_kernel,
        in_specs=[away, away, away],
        out_specs=[whole, whole],
        out_shape=[jax.ShapeDtypeStruct((EMB + VECS + 16, HALO), bf16)] * 2,
        scratch_shapes=[pltpu.VMEM((2, 1, HALO), jnp.int32), pltpu.SemaphoreType.DMA((2, 3))],
        compiler_params=pltpu.CompilerParams(vmem_limit_bytes=VMEM_BYTES),
        name="edges",
    )(emb, ids, start)


INSIDE = 2 * HALO
ENDS = 2 * (HALO + INSIDE)
END_BLOCKS = ENDS // BAND


def ends_kernel(
    low_ref, high_ref, sums_ref, id_hbm, emb_hbm, start_hbm, level_in,
    level_hbm, gram_ref,
    id_ref, emb_ref, lhs_ref, rhs_ref, weight_ref, scale_ref, start_ref, pack_a, pack_b, level_a, level_b, sems,
):
    rows = emb_hbm.shape[1]
    first = slice(0, INSIDE)
    last = slice(rows - INSIDE, rows)
    first_at = slice(HALO, HALO + INSIDE)
    last_at = slice(HALO + INSIDE, HALO + 2 * INSIDE)
    copies = [
        pltpu.make_async_copy(source.at[:, there], target.at[:, here], sems.at[i])
        for i, (source, there, target, here) in enumerate(
            (
                (id_hbm, first, id_ref, first_at),
                (id_hbm, last, id_ref, last_at),
                (emb_hbm, first, emb_ref, first_at),
                (emb_hbm, last, emb_ref, last_at),
                (start_hbm, first, start_ref, first_at),
                (start_hbm, last, start_ref, last_at),
            )
        )
    ]
    for copy in copies:
        copy.start()
    for ref, begin in ((low_ref, 0), (high_ref, ENDS - HALO)):
        here = slice(begin, begin + HALO)
        emb_ref[:, here] = ref[:EMB, :]
        start_ref[:, here] = ref[EMB : EMB + VECS, :]
        id_ref[:, here] = ref[EMB + VECS :, :].astype(f32)[:1].astype(jnp.int32) - 1
    for copy in copies[:4]:
        copy.wait()
    for j in range(ENDS // 256):
        here = slice(j * 256, j * 256 + 256)
        prepare(emb_ref[:, here], id_ref[:, here] + 1, 2 * j, lhs_ref, rhs_ref)
    carried = jnp.zeros((1, BAND), f32)
    for i in range(END_BLOCKS // 2):
        carried = affinity_pair(
            2 * i, 2 * i, carried, i < END_BLOCKS // 2 - 1, lhs_ref, rhs_ref, weight_ref, scale_ref
        )
    pack0, level1, level2, level3, products = operators(
        lambda b: b * BAND, weight_ref, scale_ref, start_ref, pack_a, pack_b, level_a, level_b
    )
    half = END_BLOCKS // 2
    for copy in copies[4:]:
        copy.wait()
    for margin, one in ((1, pack0), (2, level1), (3, level2), (4, level3)):
        for b in (*range(margin, half - margin), *range(half + margin, END_BLOCKS - margin)):
            one(b)
    outs = [
        pltpu.make_async_copy(level_a.at[:, here], level_hbm.at[:, there], sems.at[i])
        for i, (here, there) in enumerate(
            (
                (slice(HALO, 2 * HALO), slice(0, HALO)),
                (slice(ENDS - 2 * HALO, ENDS - HALO), slice(rows - HALO, rows)),
            )
        )
    ]
    for copy in outs:
        copy.start()
    sums = products(HALO_BLOCKS, HALO_BLOCKS) + products(END_BLOCKS - 2 * HALO_BLOCKS, HALO_BLOCKS)
    gram_ref[...] = sums_ref[...] + combine(sums)
    for copy in outs:
        copy.wait()


def ends(low, high, ids, sums, emb, start, level):
    whole = pl.BlockSpec(memory_space=pltpu.VMEM)
    away = pl.BlockSpec(memory_space=pl.ANY)
    return pl.pallas_call(
        ends_kernel,
        in_specs=[whole, whole, whole, away, away, away, away],
        out_specs=[away, whole],
        out_shape=[
            jax.ShapeDtypeStruct(level.shape, f32),
            jax.ShapeDtypeStruct((VECS, 2 * VECS), f32),
        ],
        input_output_aliases={6: 0},
        scratch_shapes=[
            pltpu.VMEM((1, ENDS), jnp.int32),
            pltpu.VMEM((EMB, ENDS), bf16),
            pltpu.VMEM((DEPTH, ENDS), bf16),
            pltpu.VMEM((DEPTH, ENDS), bf16),
            pltpu.VMEM((END_BLOCKS, 3 * BAND, BAND), bf16),
            pltpu.VMEM((1, ENDS), f32),
            pltpu.VMEM((VECS, ENDS), bf16),
            pltpu.VMEM((VECS, ENDS), bf16),
            pltpu.VMEM((VECS, ENDS), bf16),
            pltpu.VMEM((VECS, ENDS), f32),
            pltpu.VMEM((VECS, ENDS), f32),
            pltpu.SemaphoreType.DMA((6,)),
        ],
        compiler_params=pltpu.CompilerParams(vmem_limit_bytes=VMEM_BYTES),
        name="ends",
    )(low, high, sums, ids, emb, start, level)


def total(x, axes):
    size = lax.axis_size(axes)
    minor = lax.axis_size(axes[-1])
    if size & (size - 1):
        return lax.psum(x, axes)

    def partner(bits):
        return lax.ppermute(x, axes, [(i, i ^ bits) for i in range(size)])

    strides = [1 << k for k in range(size.bit_length() - 1)]
    strides = [s for s in strides if s >= minor] + [s for s in strides if s < minor]
    if len(strides) % 2:
        x = x + partner(strides.pop(0))
    for one, two in zip(strides[::2], strides[1::2]):
        x = (x + partner(one)) + (partner(two) + partner(one ^ two))
    return x


def basis_kernel(gram_ref, level_hbm, basis_ref, ritz_ref, inverse_ref, level_ref, sems):
    step = pl.program_id(0)
    width = basis_ref.shape[1]

    def fetch(i):
        here = columns(i * width, width)
        return pltpu.make_async_copy(level_hbm.at[:, here], level_ref.at[:, here], sems.at[i])

    @pl.when(step == 0)
    def _():
        for i in range(level_ref.shape[1] // width):
            fetch(i).start()
        row = lax.broadcasted_iota(jnp.int32, (VECS, 2 * VECS), 0)
        col = lax.broadcasted_iota(jnp.int32, (VECS, 2 * VECS), 1)
        work = jnp.where(col < VECS, gram_ref[...], jnp.where(col == row + VECS, 1.0, 0.0))
        for k in range(0, VECS, GROUP):
            spread = [jnp.broadcast_to(work[:, j : j + 1], work.shape) for j in range(k, k + GROUP)]
            pivots = [work[j : j + 1, :] for j in range(k, k + GROUP)]
            for j in range(GROUP):
                factor = jnp.where(row > k + j, spread[j] * (1.0 / spread[j][k + j : k + j + 1, :]), 0.0)
                for m in range(j + 1, GROUP):
                    spread[m] = spread[m] - factor * spread[m][k + j : k + j + 1, :]
                    pivots[m] = pivots[m] - factor[k + m : k + m + 1, :] * pivots[j]
                work = work - factor * pivots[j]
        diagonal = jnp.sum(jnp.where(row == col, work, 0.0), axis=1, keepdims=True)
        inverse = (work * lax.rsqrt(diagonal))[:, VECS:]
        image = gram_ref[:, VECS:]
        exact = lax.Precision.HIGHEST
        left = jnp.dot(inverse, image, precision=exact, preferred_element_type=f32)
        ritz_ref[...] = lax.dot_general(
            left, inverse, (((1,), (1,)), ((), ())), precision=exact, preferred_element_type=f32
        )
        high, low = split(inverse)
        inverse_ref[...] = jnp.concatenate([high, high, low], axis=1)

    fetch(step).wait()
    high, low = split(level_ref[:, columns(step * width, width)])
    basis_ref[...] = jnp.dot(
        inverse_ref[...], jnp.concatenate([high, low, high], axis=0), preferred_element_type=f32
    )


def orthonormal(sums, level):
    rows = level.shape[1]
    width = 2 * CHUNK
    whole = pl.BlockSpec(memory_space=pltpu.VMEM)
    return pl.pallas_call(
        basis_kernel,
        grid=(rows // width,),
        in_specs=[whole, pl.BlockSpec(memory_space=pl.ANY)],
        out_specs=[pl.BlockSpec((VECS, width), lambda i: (0, i)), whole],
        out_shape=[
            jax.ShapeDtypeStruct((VECS, rows), f32),
            jax.ShapeDtypeStruct((VECS, VECS), f32),
        ],
        scratch_shapes=[
            pltpu.VMEM((VECS, 3 * VECS), bf16),
            pltpu.VMEM((VECS, rows), f32),
            pltpu.SemaphoreType.DMA((rows // width,)),
        ],
        compiler_params=pltpu.CompilerParams(vmem_limit_bytes=VMEM_BYTES),
        name="basis",
    )(sums, level)


def per_device(embeddings, stream_ids, start_block):
    emb, start = embeddings.T, start_block.T
    rows = emb.shape[1]
    ids = stream_ids.reshape(1, rows)

    first, last = edges(emb, ids, start)
    axes = ("ta", "au")
    steps = range(lax.axis_size(axes) - 1)
    low = lax.ppermute(last, axes, [(i, i + 1) for i in steps])
    high = lax.ppermute(first, axes, [(i + 1, i) for i in steps])
    level, sums = interior(emb, ids, start)
    level, sums = ends(low, high, ids, sums, emb, start, level)
    basis, ritz = orthonormal(total(sums, axes), level)
    return basis.T, ritz


def solution(mesh):
    placed = (P(("ta", "au"), None), P(("ta", "au")), P(("ta", "au"), None))
    return jax.shard_map(
        per_device,
        mesh=mesh,
        in_specs=placed,
        out_specs=(P(("ta", "au"), None), P()),
        check_vma=False,
    )
```
